512 devices in a mesh: ctx: 64 (over z_lo, y, core), ch: 8 (over z_hi, x).
Axes of the slice: x: 4, y: 8, z: 8 (z_hi: 2, z_lo: 4; z = z_hi * 4 + z_lo), core: 2. Of those that a mesh axis runs over, the one named last changes fastest.
Arguments:
- cotangent: bfloat16 [8192, 4096], P('ctx', 'ch'), may hold values from -6 to 6
- out_weight: bfloat16 [4096, 4096], P('ch', 'ctx'), may hold values from -0.09375 to 0.09375
- gate_value: float32 [8192, 4096], P('ctx', 'ch'), may hold values from -6 to 6
- conv_output: float32 [8192, 4096], P('ctx', 'ch'), may hold values from -6 to 6
- conv_input: float32 [8192, 4096], P('ctx', 'ch'), may hold values from -6 to 6
- filters: float32 [256, 2048], P('ch'), may hold values from -1 to 1
Outputs:
- input_grad: float32 [8192, 4096], P('ctx', 'ch')
- gate_grad: float32 [8192, 4096], P('ctx', 'ch')
- filter_grad: float32 [256, 2048], P('ch', 'ctx')
The draws below stay inside these ranges and needn't reach their ends.
All inputs are finite; a program needn't handle non-finite values.
Results may differ from the reference program's by a relative error of at most 0.0003.
Values may be sent and summed in bfloat16 or wider, within the bound.
A program may use at most 64 MiB of HBM per device.

```python
import math
import jax
import jax.numpy as jnp
from jax import lax

TOK_DEV = 128
GROUPS = 256
GROUP_CH = 16
LAGS = 2048
D = 4096
TOKENS = 8192


def draw_filters(key, part):
    subkeys = jax.random.split(jax.random.fold_in(key, 7), 6)
    positions = jnp.arange(LAGS).astype(jnp.float32)
    fast_limit = 5
    slow_low = 1.0
    slow_high = 6.0
    fast_group = jax.random.randint(subkeys[0], (GROUPS, 1), 0, 10) < fast_limit
    slow_decay = LAGS * jnp.exp(jax.random.uniform(subkeys[1], (GROUPS, 1), minval=math.log(slow_low), maxval=math.log(slow_high)))
    fast_decay = TOK_DEV * jax.random.uniform(subkeys[2], (GROUPS, 1), minval=0.25, maxval=0.4)
    decay = jnp.where(fast_group, fast_decay, slow_decay)
    envelope = jnp.exp(-positions[None, :] / decay)
    spots = jax.random.randint(subkeys[3], (GROUPS, 2, 1), 1, LAGS)
    drops = jax.random.uniform(subkeys[4], (GROUPS, 2, 1), minval=0.6, maxval=0.8)
    envelope = envelope * jnp.prod(jnp.where(positions[None, None, :] >= spots.astype(jnp.float32), drops, 1.0), axis=1)
    raw_taps = jax.random.normal(subkeys[5], (GROUPS, LAGS)) * envelope
    return raw_taps / jnp.sqrt(jnp.sum(raw_taps * raw_taps, axis=1, keepdims=True))


def block_levels(rng, dims, pieces, low, largest):
    factor_of, own = 1.0, jax.random.fold_in(rng, 6)
    for position, blocks in pieces:
        draws = jnp.exp(jax.random.uniform(jax.random.fold_in(own, position), (blocks,), jnp.float32, low / len(pieces), largest / len(pieces)))
        factor_of = factor_of * jnp.repeat(draws, dims[position] // blocks).reshape([-1 if axis == position else 1 for axis in range(len(dims))])
    return factor_of


def gaussian(rng, shape, spread, most, cuts=(), dtype=jnp.bfloat16):
    drawn = spread * jax.random.normal(rng, shape, jnp.float32)
    if cuts:
        drawn = drawn * block_levels(rng, shape, cuts, -0.22, 0.18)
    return jnp.clip(drawn, -most, most).astype(dtype)


def setup_inputs(seed: int = 0) -> dict:
    key_of = jax.random.split(jax.random.key(seed), 7)
    cotangent = gaussian(key_of[0], (TOKENS, D), 1.0, 6.0, ((0, 64), (1, 8)))
    out_weight = gaussian(key_of[1], (D, D), D ** -0.5, 0.09375, ((0, 8), (1, 64)))
    gate_value = gaussian(key_of[2], (TOKENS, D), 1.0, 6.0, ((0, 64), (1, 8)), jnp.float32)
    conv_output = gaussian(key_of[3], (TOKENS, D), 1.0, 6.0, ((0, 64), (1, 8)), jnp.float32)
    conv_input = gaussian(key_of[4], (TOKENS, D), 1.0, 6.0, ((0, 64), (1, 8)), jnp.float32)
    filters = draw_filters(jax.random.fold_in(key_of[6], 71), 0)
    return {"cotangent": cotangent, "out_weight": out_weight, "gate_value": gate_value, "conv_output": conv_output, "conv_input": conv_input, "filters": filters}


def reference(cotangent, out_weight, gate_value, conv_output, conv_input, filters):
    grad_out = jnp.dot(cotangent, out_weight.T, preferred_element_type=jnp.float32)
    gate_grad = grad_out * conv_output
    seq_grad = grad_out * gate_value
    fft_length = TOKENS + LAGS
    group_batch = math.gcd(GROUPS, 16)
    batch_count = GROUPS // group_batch
    width = group_batch * GROUP_CH
    grad_blocks = seq_grad.reshape(TOKENS, batch_count, width).transpose(1, 0, 2)
    input_blocks = conv_input.reshape(TOKENS, batch_count, width).transpose(1, 0, 2)
    filter_blocks = filters.reshape(batch_count, group_batch, LAGS)

    def per_block(operands):
        grad_rows, input_rows, filter_rows = operands
        grad_spectrum = jnp.fft.rfft(grad_rows, n=fft_length, axis=0)
        input_spectrum = jnp.fft.rfft(input_rows, n=fft_length, axis=0)
        filter_spectrum = jnp.fft.rfft(filter_rows, n=fft_length, axis=1)
        channel_spectrum = jnp.repeat(filter_spectrum.T, GROUP_CH, axis=1)
        input_part = jnp.fft.irfft(grad_spectrum * jnp.conj(channel_spectrum), n=fft_length, axis=0)[:TOKENS]
        cross_spectrum = (grad_spectrum * jnp.conj(input_spectrum)).reshape(-1, group_batch, GROUP_CH).sum(axis=2)
        lag_part = jnp.fft.irfft(cross_spectrum, n=fft_length, axis=0)[:LAGS].T
        return (input_part.astype(jnp.float32), lag_part.astype(jnp.float32))
    input_parts, lag_parts = lax.map(per_block, (grad_blocks, input_blocks, filter_blocks))
    input_grad = input_parts.transpose(1, 0, 2).reshape(TOKENS, D)
    filter_grad = lag_parts.reshape(GROUPS, LAGS) * (1.0 / math.sqrt(GROUP_CH * TOKENS))
    return (input_grad, gate_grad, filter_grad)
```

```python
import functools
import math

import jax
import jax.numpy as jnp
from jax import lax
from jax.experimental import pallas as pl
from jax.experimental.pallas import tpu as pltpu
from jax.sharding import PartitionSpec as P

MESH = pl.DeviceIdType.MESH
F32, BF16 = jnp.float32, jnp.bfloat16
NT = (((1,), (1,)), ((), ()))
NN = (((1,), (0,)), ((), ()))
GRID = {"z_lo": 4, "y": 8, "z_hi": 2, "x": 4}
TOK = 128
BLOCK = 2 * TOK
ROWS = 8


def split(value):
    high = value.astype(BF16)
    return high, (value - high.astype(F32)).astype(BF16)


def mm(a, b, dims):
    return lax.dot_general(a, b, dims, preferred_element_type=F32)


def mm3(a, b, dims):
    return mm(a[0], b[0], dims) + (mm(a[0], b[1], dims) + mm(a[1], b[0], dims))


def kernel(
    dims, scale,
    cot_ref, w_ref, gate_ref, cout_ref, cin_ref, filt_ref,
    ig_ref, gg_ref, fg_ref,
    wfull, cotfull, xt, xb, st, sb, outt, rt, tap_hi, tap_lo, xr_hi, xr_lo, corr, fgs, fgr, grad,
    w_send, w_recv, c_send, c_recv, x_sem, s_sem, o_sem, f_sem,
):
    zl_n, y_n, zh_n, x_n, lag_blocks = dims
    chips = zl_n * y_n
    n_ctx = 2 * chips
    me = lax.axis_index("ctx")
    core = lax.rem(me, 2)
    chip = lax.div(me, 2)
    y = lax.rem(chip, y_n)
    zl = lax.div(chip, y_n)
    mej = lax.axis_index("ch")
    x = lax.rem(mej, x_n)
    zh = lax.div(mej, x_n)
    sibling = me + 1 - 2 * core
    x_near = ([lax.rem(x + 1, x_n), lax.rem(x + x_n - 1, x_n)] if x_n > 1 else [])

    def ctx_of(z_, y_, c_):
        return (z_ * y_n + y_) * 2 + c_

    def remote(src, dst, send, recv, **where):
        return pltpu.make_async_remote_copy(
            src_ref=src, dst_ref=dst, send_sem=send, recv_sem=recv,
            device_id=where, device_id_type=MESH,
        )

    barrier = pltpu.get_barrier_semaphore()

    def greet(k, carry):
        pl.semaphore_signal(barrier, inc=1, device_id={"ctx": lax.rem(me + k, n_ctx)}, device_id_type=MESH)
        return carry

    lax.fori_loop(1, n_ctx, greet, 0)
    for near in x_near:
        pl.semaphore_signal(barrier, inc=1, device_id={"ch": zh * x_n + near}, device_id_type=MESH)
    if zh_n > 1:
        pl.semaphore_signal(barrier, inc=1, device_id={"ch": (1 - zh) * x_n + x}, device_id_type=MESH)

    depth = w_ref.shape[1]
    eye = (lax.broadcasted_iota(jnp.int32, (depth, depth), 0) == lax.broadcasted_iota(jnp.int32, (depth, depth), 1))
    wfull[me] = mm(eye.astype(F32).astype(BF16), w_ref[...], NT).astype(BF16)
    cotfull[mej] = cot_ref[...]
    xt[...] = jnp.transpose(cin_ref[...]).reshape(n_ctx, ROWS, TOK)
    sb[:, chips:] = jnp.zeros((2, lag_blocks, ROWS, TOK), F32)

    pl.semaphore_wait(barrier, (n_ctx - 1) + len(x_near) + (zh_n - 1))

    def w_copy(piece, target):
        return remote(wfull.at[piece], wfull.at[piece], w_send, w_recv.at[piece], ctx=target)

    up = ctx_of(zl, lax.rem(y + 1, y_n), core)
    down = ctx_of(zl, lax.rem(y + y_n - 1, y_n), core)
    half = y_n // 2
    z_of = [lax.rem(zl + k, zl_n) for k in range(zl_n)]

    def goes_up(distance, k):
        return distance < half or (distance == half and k < zl_n // 2)

    def goes_down(distance, k):
        return distance < half or (distance == half and k >= zl_n // 2)

    def w_relay(piece, distance, k, to_up, to_down):
        if to_up and goes_up(distance, k):
            w_copy(piece, up).start()
        if to_down and goes_down(distance, k):
            w_copy(piece, down).start()
        w_copy(piece, sibling).start()

    for k in range(1, zl_n):
        w_copy(me, ctx_of(z_of[k], y, core)).start()
    w_relay(me, 1, 0, y_n > 1, y_n > 1)

    def c_copy(src, plane, xx, rows, sem, near):
        piece = plane * x_n + xx
        return remote(src, cotfull.at[piece, rows], c_send, c_recv.at[piece, sem], ch=plane_target(near))

    def plane_target(near):
        return zh * x_n + near

    everything, low, high = pl.ds(0, TOK), pl.ds(0, TOK // 2), pl.ds(TOK // 2, TOK // 2)

    def c_spread(src, plane):
        for near in x_near:
            c_copy(src.at[everything], plane, x, everything, 0, near).start()

    def c_forward(plane):
        if x_n == 1:
            return
        right, left = x_near
        for source, rows, sem, target in ((left, low, 0, right), (right, high, 1, left)):
            piece = plane * x_n + source
            c_copy(cotfull.at[piece, everything], plane, source, everything, 0, target).wait_recv()
            c_copy(cotfull.at[piece, rows], plane, source, rows, sem, target).start()

    def c_finish(plane):
        if x_n == 1:
            return
        far = lax.rem(x + 2, x_n)
        for rows, sem in ((low, 0), (high, 1)):
            c_copy(cotfull.at[plane * x_n + far, rows], plane, far, rows, sem, far).wait_recv()

    def c_across():
        return remote(cot_ref, cotfull.at[mej], c_send, c_recv.at[mej, 0], ch=(1 - zh) * x_n + x)

    c_spread(cot_ref, zh)
    if zh_n > 1:
        c_across().start()

    def slot_of(target):
        return lax.rem(target, 2) * chips + lax.div(target, 2)

    def x_send(k, carry):
        target = lax.rem(me + k, n_ctx)
        remote(xt.at[slot_of(target)], xb.at[core, chip], x_sem.at[0], x_sem.at[1], ctx=target).start()
        return carry

    lax.fori_loop(1, n_ctx, x_send, 0)
    pltpu.make_async_copy(xt.at[slot_of(me)], xb.at[core, chip], x_sem.at[1]).start()

    for k in range(1, zl_n):
        piece = ctx_of(z_of[k], y, core)
        w_copy(piece, sibling).wait_recv()
        w_relay(piece, 1, k, y_n > 1, y_n > 1)
    c_forward(zh)

    group = core * (chips // 2) + lax.div(chip, 2)
    wide = tap_hi.shape[1]
    row = jnp.pad(filt_ref[pl.ds(group, 1), :], ((0, 0), (0, wide - filt_ref.shape[1])))
    taps = pltpu.roll(jnp.broadcast_to(row, (BLOCK, wide)), 0, 1, stride=1, stride_axis=0)
    tap_hi[...], tap_lo[...] = split(taps)

    def w_step(s):
        for k in range(zl_n):
            if goes_up(s, k):
                piece = ctx_of(z_of[k], lax.rem(y + y_n - s, y_n), core)
                w_copy(piece, sibling).wait_recv()
                w_relay(piece, s + 1, k, True, False)
            if goes_down(s, k):
                piece = ctx_of(z_of[k], lax.rem(y + s, y_n), core)
                w_copy(piece, sibling).wait_recv()
                w_relay(piece, s + 1, k, False, True)

    for s in range(1, half + 1):
        w_step(s)
        if zh_n > 1 and s == max(half - 2, 1):
            other = (1 - zh) * x_n + x
            remote(cotfull.at[other], cotfull.at[other], c_send, c_recv.at[other, 0], ch=mej).wait_recv()
            c_spread(cotfull.at[other], 1 - zh)
    if zh_n > 1:
        if half == 0:
            other = (1 - zh) * x_n + x
            remote(cotfull.at[other], cotfull.at[other], c_send, c_recv.at[other, 0], ch=mej).wait_recv()
            c_spread(cotfull.at[other], 1 - zh)
        c_forward(1 - zh)

    pltpu.make_async_copy(xb, xb, x_sem.at[1]).wait()
    turn = (
        lax.broadcasted_iota(jnp.int32, (BLOCK, BLOCK), 0) + lax.broadcasted_iota(jnp.int32, (BLOCK, BLOCK), 1) == BLOCK - 1
    ).astype(F32).astype(BF16)
    x_all = jnp.concatenate([xb[0].reshape(chips * ROWS, TOK), xb[1].reshape(chips * ROWS, TOK)], axis=1)
    x_hi, x_lo = split(x_all)
    xr_hi[...] = mm(turn, x_hi, NT).astype(BF16)
    xr_lo[...] = mm(turn, x_lo, NT).astype(BF16)

    c_finish(zh)
    if zh_n > 1:
        c_finish(1 - zh)

    def from_sibling(q, carry):
        w_copy(2 * q + 1 - core, sibling).wait_recv()
        return carry

    lax.fori_loop(0, chips, from_sibling, 0)

    per = n_ctx // (zh_n * x_n)
    for j in range(zh_n * x_n):
        term = mm(cotfull[j], wfull[pl.ds(j * per, per)].reshape(per * depth, wfull.shape[2]), NN)
        if j == 0:
            grad[...] = term
        else:
            grad[...] += term
    st[...] = jnp.transpose(grad[...] * gate_ref[...]).reshape(n_ctx, ROWS, TOK)

    def s_send(k, carry):
        target = lax.rem(me + k, n_ctx)
        remote(st.at[slot_of(target)], sb.at[core, chip], s_sem.at[0], s_sem.at[1], ctx=target).start()
        return carry

    lax.fori_loop(1, n_ctx, s_send, 0)
    pltpu.make_async_copy(st.at[slot_of(me)], sb.at[core, chip], s_sem.at[1]).start()
    gg_ref[...] = grad[...] * cout_ref[...]
    arrived = sb.at[:, pl.ds(0, chips)]
    pltpu.make_async_copy(arrived, arrived, s_sem.at[1]).wait()

    total = jnp.zeros((chips * ROWS, BLOCK), F32)
    for d in range(lag_blocks + 1):
        s_rows = jnp.concatenate(
            [sb[0, d : d + chips].reshape(chips * ROWS, TOK), sb[1, d : d + chips].reshape(chips * ROWS, TOK)], axis=1
        )
        s_pair = split(s_rows)
        cols = slice(d * BLOCK, (d + 1) * BLOCK)
        total = total + mm3(s_pair, (tap_hi[:, cols], tap_lo[:, cols]), NT)
        corr[:, cols] = mm3((xr_hi[...], xr_lo[...]), s_pair, NN)
    for c in range(2):
        outt[c] = total[:, c * TOK : (c + 1) * TOK].reshape(chips, ROWS, TOK)

    def o_send(k, carry):
        target = lax.rem(me + k, n_ctx)
        remote(
            outt.at[lax.rem(target, 2), lax.div(target, 2)], rt.at[slot_of(me)], o_sem.at[0], o_sem.at[1], ctx=target
        ).start()
        return carry

    lax.fori_loop(1, n_ctx, o_send, 0)
    pltpu.make_async_copy(outt.at[core, chip], rt.at[slot_of(me)], o_sem.at[1]).start()

    lined = pltpu.roll(corr[...], wide - (BLOCK - 1), 1, stride=1, stride_axis=0)
    lags = jnp.sum(lined, axis=0, keepdims=True) * scale
    for s in range(fgs.shape[0]):
        fgs[s] = lags[:, s * TOK : (s + 1) * TOK]
    place = lax.rem(chip, 2) * chips + core * (chips // 2) + lax.div(chip, 2)
    share = fg_ref.shape[1]

    def f_send(k, carry):
        target = lax.rem(me + k, n_ctx)
        remote(
            fgs.at[lax.div(target * share, TOK)], fgr.at[place], f_sem.at[0], f_sem.at[1], ctx=target
        ).start()
        return carry

    lax.fori_loop(1, n_ctx, f_send, 0)
    pltpu.make_async_copy(fgs.at[lax.div(me * share, TOK)], fgr.at[place], f_sem.at[1]).start()

    pltpu.make_async_copy(rt, rt, o_sem.at[1]).wait()
    ig_ref[...] = jnp.transpose(rt[...].reshape(n_ctx * ROWS, TOK))
    pltpu.make_async_copy(fgr, fgr, f_sem.at[1]).wait()
    parts = fgr[...].reshape(n_ctx, TOK)
    both = parts[:chips] + parts[chips:]
    offset = lax.rem(me * share, TOK)
    fg_ref[...] = pltpu.roll(both, lax.rem(TOK - offset, TOK), 1)[:, :share]

    pltpu.make_async_copy(wfull.at[pl.ds(0, n_ctx - 1)], wfull.at[pl.ds(0, n_ctx - 1)], w_send).wait()
    if zh_n * x_n > 1:
        sent = cotfull.at[pl.ds(0, zh_n * x_n - 1)]
        pltpu.make_async_copy(sent, sent, c_send).wait()
    for ref, sem in ((xt, x_sem), (st, s_sem), (rt, o_sem), (fgr, f_sem)):
        part = ref.at[pl.ds(0, n_ctx - 1)]
        pltpu.make_async_copy(part, part, sem.at[0]).wait()


def shards(grid, cotangent, out_weight, gate_value, conv_output, conv_input, filters):
    tokens, channels = gate_value.shape
    groups, lag_count = filters.shape
    n_ctx, n_ch = lax.axis_size("ctx"), lax.axis_size("ch")
    chips = n_ctx // 2
    lag_blocks = -(-lag_count // BLOCK)
    wide = (lag_blocks + 1) * BLOCK
    segments = -(-lag_count // TOK)
    scale = 1.0 / math.sqrt(channels // groups * tokens * n_ctx)
    dims = (grid["z_lo"], grid["y"], grid["z_hi"], grid["x"], lag_blocks)
    vmem = pl.BlockSpec(memory_space=pltpu.VMEM)
    dma = pltpu.SemaphoreType.DMA
    return pl.pallas_call(
        functools.partial(kernel, dims, scale),
        out_shape=(
            jax.ShapeDtypeStruct((tokens, channels), F32),
            jax.ShapeDtypeStruct((tokens, channels), F32),
            jax.ShapeDtypeStruct((groups, lag_count // n_ctx), F32),
        ),
        in_specs=[vmem] * 6,
        out_specs=(vmem,) * 3,
        scratch_shapes=[
            pltpu.VMEM((n_ctx, out_weight.shape[1], channels), BF16),
            pltpu.VMEM((n_ch, tokens, channels), BF16),
            pltpu.VMEM((n_ctx, ROWS, TOK), F32),
            pltpu.VMEM((2, chips, ROWS, TOK), F32),
            pltpu.VMEM((n_ctx, ROWS, TOK), F32),
            pltpu.VMEM((2, chips + lag_blocks, ROWS, TOK), F32),
            pltpu.VMEM((2, chips, ROWS, TOK), F32),
            pltpu.VMEM((n_ctx, ROWS, TOK), F32),
            pltpu.VMEM((BLOCK, wide), BF16),
            pltpu.VMEM((BLOCK, wide), BF16),
            pltpu.VMEM((BLOCK, chips * ROWS), BF16),
            pltpu.VMEM((BLOCK, chips * ROWS), BF16),
            pltpu.VMEM((BLOCK, wide), F32),
            pltpu.VMEM((segments, 1, TOK), F32),
            pltpu.VMEM((n_ctx, 1, TOK), F32),
            pltpu.VMEM((tokens, channels), F32),
            dma,
            dma((n_ctx,)),
            dma,
            dma((n_ch, 2)),
            dma((2,)),
            dma((2,)),
            dma((2,)),
            dma((2,)),
        ],
        compiler_params=pltpu.CompilerParams(
            collective_id=0, has_side_effects=True, vmem_limit_bytes=48 * 1024 * 1024
        ),
    )(cotangent, out_weight, gate_value, conv_output, conv_input, filters)


def solution(mesh, grid=GRID):
    return jax.shard_map(
        functools.partial(shards, grid),
        mesh=mesh,
        in_specs=(
            P("ctx", "ch"),
            P("ch", "ctx"),
            P("ctx", "ch"),
            P("ctx", "ch"),
            P("ctx", "ch"),
            P("ch", None),
        ),
        out_specs=(P("ctx", "ch"), P("ctx", "ch"), P("ch", "ctx")),
        check_vma=False,
    )
```

```python
import functools
import math

import jax
import jax.numpy as jnp
from jax import lax
from jax.experimental import pallas as pl
from jax.experimental.pallas import tpu as pltpu
from jax.sharding import PartitionSpec as P

MESH = pl.DeviceIdType.MESH
F32, BF16 = jnp.float32, jnp.bfloat16
NT = (((1,), (1,)), ((), ()))
NN = (((1,), (0,)), ((), ()))
GRID = {"z_lo": 4, "y": 8, "z_hi": 2, "x": 4}
TOK = 128
BLOCK = 2 * TOK
ROWS = 8


def split(value):
    high = value.astype(BF16)
    return high, (value - high.astype(F32)).astype(BF16)


def mm(a, b, dims):
    return lax.dot_general(a, b, dims, preferred_element_type=F32)


def mm3(a, b, dims):
    return mm(a[0], b[0], dims) + (mm(a[0], b[1], dims) + mm(a[1], b[0], dims))


def kernel(
    dims, scale,
    cot_hbm, w_hbm, gate_hbm, cout_hbm, cin_hbm, filt_hbm,
    ig_ref, gg_ref, fg_ref,
    gate_ref, cout_ref, cin_ref, filt_ref, wfull, cotfull, xt, xb, st, sb, outt, rt, tap_hi, tap_lo, xr_hi, xr_lo, corr, fgs, fgr, grad,
    w_send, w_recv, c_send, c_recv, x_sem, s_sem, o_sem, f_sem, in_sem,
):
    zl_n, y_n, zh_n, x_n, lag_blocks = dims
    chips = zl_n * y_n
    n_ctx = 2 * chips
    me = lax.axis_index("ctx")
    core = lax.rem(me, 2)
    chip = lax.div(me, 2)
    y = lax.rem(chip, y_n)
    zl = lax.div(chip, y_n)
    mej = lax.axis_index("ch")
    x = lax.rem(mej, x_n)
    zh = lax.div(mej, x_n)
    sibling = me + 1 - 2 * core
    x_far = [lax.rem(x + k, x_n) for k in (1, 3, 2) if k < x_n]

    def ctx_of(z_, y_, c_):
        return (z_ * y_n + y_) * 2 + c_

    def remote(src, dst, send, recv, **where):
        return pltpu.make_async_remote_copy(
            src_ref=src, dst_ref=dst, send_sem=send, recv_sem=recv,
            device_id=where, device_id_type=MESH,
        )

    def everyone(send):
        for dy in sorted(range(y_n), key=lambda k: -min(k, y_n - k)):
            for dz in range(zl_n):
                for other in (True, False):
                    if dy or dz or other:
                        c_ = 1 - core if other else core
                        chip_ = z_of[dz] * y_n + y_of[dy]
                        send(2 * chip_ + c_, c_, chip_, c_ * chips + chip_)

    home = core * chips + chip

    barrier = pltpu.get_barrier_semaphore()

    half = y_n // 2
    z_of = [lax.rem(zl + k, zl_n) for k in range(zl_n)]
    y_of = [lax.rem(y + k, y_n) for k in range(y_n)]
    up, down = (ctx_of(zl, y_of[k % y_n], core) for k in (1, y_n - 1))
    rings = [sibling] + ([up, down] if y_n > 2 else [up] * (y_n > 1)) + [ctx_of(z, y, core) for z in z_of[1:]]
    for near in rings:
        pl.semaphore_signal(barrier, inc=1, device_id={"ctx": near}, device_id_type=MESH)
    for near in x_far:
        pl.semaphore_signal(barrier, inc=1, device_id={"ch": zh * x_n + near}, device_id_type=MESH)
    if zh_n > 1:
        pl.semaphore_signal(barrier, inc=1, device_id={"ch": (1 - zh) * x_n + x}, device_id_type=MESH)

    group = core * (chips // 2) + lax.div(chip, 2)
    some = filt_ref.shape[0]
    loads = [
        pltpu.make_async_copy(src, dst, in_sem.at[n])
        for n, (src, dst) in enumerate(
            (
                (cin_hbm, cin_ref),
                (w_hbm, wfull.at[me]),
                (cot_hbm, cotfull.at[mej]),
                (filt_hbm.at[pl.ds(lax.div(group, some) * some, some)], filt_ref),
                (gate_hbm, gate_ref),
                (cout_hbm, cout_ref),
            )
        )
    ]
    for load in loads:
        load.start()
    sb[:, chips:] = jnp.zeros((2, lag_blocks, ROWS, TOK), F32)
    loads[0].wait()
    xt[...] = jnp.transpose(cin_ref[...]).reshape(n_ctx, ROWS, TOK)
    loads[1].wait()
    loads[2].wait()
    depth = w_hbm.shape[0]

    pl.semaphore_wait(barrier, len(rings) + len(x_far) + (zh_n - 1))

    def w_copy(piece, target):
        return remote(wfull.at[piece], wfull.at[piece], w_send, w_recv.at[piece], ctx=target)

    def goes_up(distance, k):
        return distance < half or (distance == half and k < zl_n // 2)

    def goes_down(distance, k):
        return distance < half or (distance == half and k >= zl_n // 2)

    def w_relay(piece, distance, k, to_up, to_down):
        if to_up and goes_up(distance, k):
            w_copy(piece, up).start()
        if to_down and goes_down(distance, k):
            w_copy(piece, down).start()
        w_copy(piece, sibling).start()

    for k in range(1, zl_n):
        w_copy(me, ctx_of(z_of[k], y, core)).start()
    w_relay(me, 1, 0, y_n > 1, y_n > 1)

    def c_copy(piece, xx):
        return remote(cotfull.at[piece], cotfull.at[piece], c_send, c_recv.at[piece], ch=zh * x_n + xx)

    def c_spread(piece):
        for xx in x_far:
            c_copy(piece, xx).start()

    across = (1 - zh) * x_n + x
    if zh_n > 1:
        remote(cotfull.at[mej], cotfull.at[mej], c_send, c_recv.at[mej], ch=across).start()
    c_spread(mej)

    loads[3].wait()
    wide = tap_hi.shape[1]
    row = jnp.pad(filt_ref[pl.ds(lax.rem(group, some), 1), :], ((0, 0), (0, wide - filt_ref.shape[1])))
    taps = pltpu.roll(jnp.broadcast_to(row, (BLOCK, wide)), 0, 1, stride=1, stride_axis=0)
    tap_hi[...], tap_lo[...] = split(taps)

    def from_z(k):
        piece = ctx_of(z_of[k], y, core)
        w_copy(piece, sibling).wait_recv()
        w_relay(piece, 1, k, y_n > 1, y_n > 1)

    def from_y(s, k):
        if goes_up(s, k):
            piece = ctx_of(z_of[k], y_of[y_n - s], core)
            w_copy(piece, sibling).wait_recv()
            w_relay(piece, s + 1, k, True, False)
        if goes_down(s, k):
            piece = ctx_of(z_of[k], y_of[s], core)
            w_copy(piece, sibling).wait_recv()
            w_relay(piece, s + 1, k, False, True)

    if half:
        from_y(1, 0)
    for k in range(1, zl_n):
        from_z(k)
    for s in range(1, half + 1):
        if s < half:
            from_y(s + 1, 0)
        for k in range(1, zl_n):
            from_y(s, k)
        if zh_n > 1 and s == min(2, half):
            c_copy(across, x).wait_recv()
            c_spread(across)
    for piece in range(zh_n * x_n):
        first = lax.rem(mej + piece, zh_n * x_n)
        if piece and zh_n > 1:
            @pl.when(first != across)
            def _():
                c_copy(first, x).wait_recv()
        elif piece:
            c_copy(first, x).wait_recv()

    def from_sibling(q, carry):
        w_copy(2 * q + 1 - core, sibling).wait_recv()
        return carry

    lax.fori_loop(0, chips, from_sibling, 0)

    per = n_ctx // (zh_n * x_n)
    for j in range(zh_n * x_n):
        term = mm(cotfull[j], wfull[pl.ds(j * per, per)].reshape(per * depth, wfull.shape[2]), NN)
        if j == 0:
            grad[...] = term
        else:
            grad[...] += term
    loads[4].wait()
    st[...] = jnp.transpose(grad[...] * gate_ref[...]).reshape(n_ctx, ROWS, TOK)

    def s_send(target, c_, chip_, slot):
        remote(st.at[slot], sb.at[core, chip], s_sem.at[0], s_sem.at[1], ctx=target).start()

    everyone(s_send)
    pltpu.make_async_copy(st.at[home], sb.at[core, chip], s_sem.at[1]).start()

    def x_send(target, c_, chip_, slot):
        remote(xt.at[slot], xb.at[core, chip], x_sem.at[0], x_sem.at[1], ctx=target).start()

    everyone(x_send)
    pltpu.make_async_copy(xt.at[home], xb.at[core, chip], x_sem.at[1]).start()
    loads[5].wait()
    gg_ref[...] = grad[...] * cout_ref[...]
    arrived = sb.at[:, pl.ds(0, chips)]
    pltpu.make_async_copy(arrived, arrived, s_sem.at[1]).wait()

    def s_rows(d):
        return split(jnp.concatenate(
            [sb[0, d : d + chips].reshape(chips * ROWS, TOK), sb[1, d : d + chips].reshape(chips * ROWS, TOK)], axis=1
        ))

    blocks = [slice(d * BLOCK, (d + 1) * BLOCK) for d in range(lag_blocks + 1)]
    total = jnp.zeros((chips * ROWS, BLOCK), F32)
    for d, cols in enumerate(blocks):
        total = total + mm3(s_rows(d), (tap_hi[:, cols], tap_lo[:, cols]), NT)
    for c in range(2):
        outt[c] = total[:, c * TOK : (c + 1) * TOK].reshape(chips, ROWS, TOK)

    def o_send(target, c_, chip_, slot):
        remote(outt.at[c_, chip_], rt.at[home], o_sem.at[0], o_sem.at[1], ctx=target).start()

    everyone(o_send)
    pltpu.make_async_copy(outt.at[core, chip], rt.at[home], o_sem.at[1]).start()

    pltpu.make_async_copy(xb, xb, x_sem.at[1]).wait()
    turn = (
        lax.broadcasted_iota(jnp.int32, (BLOCK, BLOCK), 0) + lax.broadcasted_iota(jnp.int32, (BLOCK, BLOCK), 1) == BLOCK - 1
    ).astype(F32).astype(BF16)
    x_all = jnp.concatenate([xb[0].reshape(chips * ROWS, TOK), xb[1].reshape(chips * ROWS, TOK)], axis=1)
    x_hi, x_lo = split(x_all)
    xr_hi[...] = mm(turn, x_hi, NT).astype(BF16)
    xr_lo[...] = mm(turn, x_lo, NT).astype(BF16)

    for d, cols in enumerate(blocks):
        corr[:, cols] = mm3((xr_hi[...], xr_lo[...]), s_rows(d), NN)

    lined = pltpu.roll(corr[...], wide - (BLOCK - 1), 1, stride=1, stride_axis=0)
    lags = jnp.sum(lined, axis=0, keepdims=True) * scale
    for s in range(fgs.shape[0]):
        fgs[s] = lags[:, s * TOK : (s + 1) * TOK]
    place = lax.rem(chip, 2) * chips + core * (chips // 2) + lax.div(chip, 2)
    share = fg_ref.shape[1]

    def f_send(target, c_, chip_, slot):
        remote(fgs.at[lax.div(chip_ * (2 * share), TOK)], fgr.at[place], f_sem.at[0], f_sem.at[1], ctx=target).start()

    everyone(f_send)
    pltpu.make_async_copy(fgs.at[lax.div(chip * (2 * share), TOK)], fgr.at[place], f_sem.at[1]).start()

    pltpu.make_async_copy(rt, rt, o_sem.at[1]).wait()
    ig_ref[...] = jnp.transpose(rt[...].reshape(n_ctx * ROWS, TOK))
    pltpu.make_async_copy(fgr, fgr, f_sem.at[1]).wait()
    parts = fgr[...].reshape(n_ctx, TOK)
    both = parts[:chips] + parts[chips:]
    offset = lax.rem(me * share, TOK)
    fg_ref[...] = pltpu.roll(both, lax.rem(TOK - offset, TOK), 1)[:, :share]

    pltpu.make_async_copy(wfull.at[pl.ds(0, n_ctx - 1)], wfull.at[pl.ds(0, n_ctx - 1)], w_send).wait()
    if zh_n * x_n > 1:
        sent = cotfull.at[pl.ds(0, zh_n * x_n - 1)]
        pltpu.make_async_copy(sent, sent, c_send).wait()
    for ref, sem in ((xt, x_sem), (st, s_sem), (rt, o_sem), (fgr, f_sem)):
        part = ref.at[pl.ds(0, n_ctx - 1)]
        pltpu.make_async_copy(part, part, sem.at[0]).wait()


def shards(grid, cotangent, out_weight, gate_value, conv_output, conv_input, filters):
    tokens, channels = gate_value.shape
    groups, lag_count = filters.shape
    n_ctx, n_ch = lax.axis_size("ctx"), lax.axis_size("ch")
    chips = n_ctx // 2
    lag_blocks = -(-lag_count // BLOCK)
    wide = (lag_blocks + 1) * BLOCK
    segments = -(-lag_count // TOK)
    scale = 1.0 / math.sqrt(channels // groups * tokens * n_ctx)
    dims = (grid["z_lo"], grid["y"], grid["z_hi"], grid["x"], lag_blocks)
    vmem = pl.BlockSpec(memory_space=pltpu.VMEM)
    dma = pltpu.SemaphoreType.DMA
    return pl.pallas_call(
        functools.partial(kernel, dims, scale),
        out_shape=(
            jax.ShapeDtypeStruct((tokens, channels), F32),
            jax.ShapeDtypeStruct((tokens, channels), F32),
            jax.ShapeDtypeStruct((groups, lag_count // n_ctx), F32),
        ),
        in_specs=[pl.BlockSpec(memory_space=pltpu.HBM)] * 6,
        out_specs=(vmem,) * 3,
        scratch_shapes=[
            pltpu.VMEM((tokens, channels), F32),
            pltpu.VMEM((tokens, channels), F32),
            pltpu.VMEM((tokens, channels), F32),
            pltpu.VMEM((min(8, groups), lag_count), F32),
            pltpu.VMEM((n_ctx, out_weight.shape[1], channels), BF16),
            pltpu.VMEM((n_ch, tokens, channels), BF16),
            pltpu.VMEM((n_ctx, ROWS, TOK), F32),
            pltpu.VMEM((2, chips, ROWS, TOK), F32),
            pltpu.VMEM((n_ctx, ROWS, TOK), F32),
            pltpu.VMEM((2, chips + lag_blocks, ROWS, TOK), F32),
            pltpu.VMEM((2, chips, ROWS, TOK), F32),
            pltpu.VMEM((n_ctx, ROWS, TOK), F32),
            pltpu.VMEM((BLOCK, wide), BF16),
            pltpu.VMEM((BLOCK, wide), BF16),
            pltpu.VMEM((BLOCK, chips * ROWS), BF16),
            pltpu.VMEM((BLOCK, chips * ROWS), BF16),
            pltpu.VMEM((BLOCK, wide), F32),
            pltpu.VMEM((segments, 1, TOK), F32),
            pltpu.VMEM((n_ctx, 1, TOK), F32),
            pltpu.VMEM((tokens, channels), F32),
            dma,
            dma((n_ctx,)),
            dma,
            dma((n_ch,)),
            dma((2,)),
            dma((2,)),
            dma((2,)),
            dma((2,)),
            dma((6,)),
        ],
        compiler_params=pltpu.CompilerParams(
            collective_id=0, has_side_effects=True, vmem_limit_bytes=66_000_000
        ),
    )(cotangent, out_weight.T, gate_value, conv_output, conv_input, filters)


def solution(mesh, grid=GRID):
    return jax.shard_map(
        functools.partial(shards, grid),
        mesh=mesh,
        in_specs=(
            P("ctx", "ch"),
            P("ch", "ctx"),
            P("ctx", "ch"),
            P("ctx", "ch"),
            P("ctx", "ch"),
            P("ch", None),
        ),
        out_specs=(P("ctx", "ch"), P("ctx", "ch"), P("ch", "ctx")),
        check_vma=False,
    )
```

```python
import functools
import math

import jax
import jax.numpy as jnp
from jax import lax
from jax.experimental import pallas as pl
from jax.experimental.pallas import tpu as pltpu
from jax.sharding import PartitionSpec as P

MESH = pl.DeviceIdType.MESH
F32, BF16 = jnp.float32, jnp.bfloat16
NT = (((1,), (1,)), ((), ()))
NN = (((1,), (0,)), ((), ()))
GRID = {"z_lo": 4, "y": 8, "z_hi": 2, "x": 4}
TOK = 128
BLOCK = 2 * TOK
ROWS = 8


def split(value):
    high = value.astype(BF16)
    return high, (value - high.astype(F32)).astype(BF16)


def mm(a, b, dims):
    return lax.dot_general(a, b, dims, preferred_element_type=F32)


def mm3(a, b, dims):
    return mm(a[0], b[0], dims) + (mm(a[0], b[1], dims) + mm(a[1], b[0], dims))


def kernel(
    dims, scale,
    cot_hbm, w_hbm, gate_hbm, cout_hbm, cin_hbm, filt_hbm,
    ig_ref, gg_ref, fg_ref,
    gate_ref, cout_ref, cin_ref, filt_ref, wfull, cotfull, xt, xb, st, sb, outt, rt, tap_hi, tap_lo, xr_hi, xr_lo, corr, fgs, fgr, grad,
    w_send, w_recv, c_send, c_recv, x_sem, s_sem, o_sem, f_sem, in_sem,
):
    zl_n, y_n, zh_n, x_n, lag_blocks = dims
    chips = zl_n * y_n
    n_ctx = 2 * chips
    me = lax.axis_index("ctx")
    core = lax.rem(me, 2)
    chip = lax.div(me, 2)
    y = lax.rem(chip, y_n)
    zl = lax.div(chip, y_n)
    mej = lax.axis_index("ch")
    x = lax.rem(mej, x_n)
    zh = lax.div(mej, x_n)
    sibling = me + 1 - 2 * core
    x_far = [lax.rem(x + k, x_n) for k in (1, 3, 2) if k < x_n]

    def ctx_of(z_, y_, c_):
        return (z_ * y_n + y_) * 2 + c_

    def remote(src, dst, send, recv, **where):
        return pltpu.make_async_remote_copy(
            src_ref=src, dst_ref=dst, send_sem=send, recv_sem=recv,
            device_id=where, device_id_type=MESH,
        )

    def everyone(send):
        for dy in sorted(range(y_n), key=lambda k: -min(k, y_n - k)):
            for dz in range(zl_n):
                for other in (True, False):
                    if dy or dz or other:
                        c_ = 1 - core if other else core
                        chip_ = z_of[dz] * y_n + y_of[dy]
                        send(2 * chip_ + c_, c_, chip_, c_ * chips + chip_)

    home = core * chips + chip

    barrier = pltpu.get_barrier_semaphore()

    half = y_n // 2
    z_of = [lax.rem(zl + k, zl_n) for k in range(zl_n)]
    y_of = [lax.rem(y + k, y_n) for k in range(y_n)]
    up, down = (ctx_of(zl, y_of[k % y_n], core) for k in (1, y_n - 1))
    rings = [sibling] + ([up, down] if y_n > 2 else [up] * (y_n > 1)) + [ctx_of(z, y, core) for z in z_of[1:]]
    for near in rings:
        pl.semaphore_signal(barrier, inc=1, device_id={"ctx": near}, device_id_type=MESH)
    for near in x_far:
        pl.semaphore_signal(barrier, inc=1, device_id={"ch": zh * x_n + near}, device_id_type=MESH)
    if zh_n > 1:
        pl.semaphore_signal(barrier, inc=1, device_id={"ch": (1 - zh) * x_n + x}, device_id_type=MESH)

    group = core * (chips // 2) + lax.div(chip, 2)
    some = filt_ref.shape[0]
    loads = [
        pltpu.make_async_copy(src, dst, in_sem.at[n])
        for n, (src, dst) in enumerate(
            (
                (cin_hbm, cin_ref),
                (w_hbm, wfull.at[me]),
                (cot_hbm, cotfull.at[mej]),
                (filt_hbm.at[pl.ds(lax.div(group, some) * some, some)], filt_ref),
                (gate_hbm, gate_ref),
                (cout_hbm, cout_ref),
            )
        )
    ]
    for load in loads:
        load.start()
    sb[:, chips:] = jnp.zeros((2, lag_blocks, ROWS, TOK), F32)
    loads[1].wait()
    loads[2].wait()
    depth = w_hbm.shape[0]

    pl.semaphore_wait(barrier, len(rings) + len(x_far) + (zh_n - 1))

    def w_copy(piece, target):
        return remote(wfull.at[piece], wfull.at[piece], w_send, w_recv.at[piece], ctx=target)

    def goes_up(distance, k):
        return distance < half or (distance == half and k < zl_n // 2)

    def goes_down(distance, k):
        return distance < half or (distance == half and k >= zl_n // 2)

    def w_relay(piece, distance, k, to_up, to_down):
        if to_up and goes_up(distance, k):
            w_copy(piece, up).start()
        if to_down and goes_down(distance, k):
            w_copy(piece, down).start()
        w_copy(piece, sibling).start()

    for k in range(1, zl_n):
        w_copy(me, ctx_of(z_of[k], y, core)).start()
    w_relay(me, 1, 0, y_n > 1, y_n > 1)

    def c_copy(piece, xx):
        return remote(cotfull.at[piece], cotfull.at[piece], c_send, c_recv.at[piece], ch=zh * x_n + xx)

    def c_spread(piece):
        for xx in x_far:
            c_copy(piece, xx).start()

    across = (1 - zh) * x_n + x
    c_spread(mej)

    def from_z(k):
        piece = ctx_of(z_of[k], y, core)
        w_copy(piece, sibling).wait_recv()
        w_relay(piece, 1, k, y_n > 1, y_n > 1)

    def from_y(s, k):
        if goes_up(s, k):
            piece = ctx_of(z_of[k], y_of[y_n - s], core)
            w_copy(piece, sibling).wait_recv()
            w_relay(piece, s + 1, k, True, False)
        if goes_down(s, k):
            piece = ctx_of(z_of[k], y_of[s], core)
            w_copy(piece, sibling).wait_recv()
            w_relay(piece, s + 1, k, False, True)

    if half:
        from_y(1, 0)
    for k in range(1, zl_n):
        from_z(k)
    if zh_n > 1:
        remote(cotfull.at[mej], cotfull.at[mej], c_send, c_recv.at[mej], ch=across).start()
    loads[3].wait()
    wide = tap_hi.shape[1]
    row = jnp.pad(filt_ref[pl.ds(lax.rem(group, some), 1), :], ((0, 0), (0, wide - filt_ref.shape[1])))
    taps = pltpu.roll(jnp.broadcast_to(row, (BLOCK, wide)), 0, 1, stride=1, stride_axis=0)
    tap_hi[...], tap_lo[...] = split(taps)

    loads[0].wait()
    xt[...] = jnp.transpose(cin_ref[...]).reshape(n_ctx, ROWS, TOK)
    for s in range(1, half + 1):
        if s < half:
            from_y(s + 1, 0)
        for k in range(1, zl_n):
            from_y(s, k)
        if zh_n > 1 and s == 1:
            c_copy(across, x).wait_recv()
            c_spread(across)
    for piece in range(zh_n * x_n):
        first = lax.rem(mej + piece, zh_n * x_n)
        if piece and zh_n > 1:
            @pl.when(first != across)
            def _():
                c_copy(first, x).wait_recv()
        elif piece:
            c_copy(first, x).wait_recv()

    def from_sibling(q, carry):
        w_copy(2 * q + 1 - core, sibling).wait_recv()
        return carry

    lax.fori_loop(0, chips, from_sibling, 0)

    per = n_ctx // (zh_n * x_n)
    for j in range(zh_n * x_n):
        term = mm(cotfull[j], wfull[pl.ds(j * per, per)].reshape(per * depth, wfull.shape[2]), NN)
        if j == 0:
            grad[...] = term
        else:
            grad[...] += term
    loads[4].wait()
    st[...] = jnp.transpose(grad[...] * gate_ref[...]).reshape(n_ctx, ROWS, TOK)

    def s_send(target, c_, chip_, slot):
        remote(st.at[slot], sb.at[core, chip], s_sem.at[0], s_sem.at[1], ctx=target).start()

    everyone(s_send)
    pltpu.make_async_copy(st.at[home], sb.at[core, chip], s_sem.at[1]).start()

    def x_send(target, c_, chip_, slot):
        remote(xt.at[slot], xb.at[core, chip], x_sem.at[0], x_sem.at[1], ctx=target).start()

    everyone(x_send)
    pltpu.make_async_copy(xt.at[home], xb.at[core, chip], x_sem.at[1]).start()
    loads[5].wait()
    gg_ref[...] = grad[...] * cout_ref[...]
    arrived = sb.at[:, pl.ds(0, chips)]
    pltpu.make_async_copy(arrived, arrived, s_sem.at[1]).wait()

    def s_rows(d):
        return split(jnp.concatenate(
            [sb[0, d : d + chips].reshape(chips * ROWS, TOK), sb[1, d : d + chips].reshape(chips * ROWS, TOK)], axis=1
        ))

    blocks = [slice(d * BLOCK, (d + 1) * BLOCK) for d in range(lag_blocks + 1)]
    total = jnp.zeros((chips * ROWS, BLOCK), F32)
    for d, cols in enumerate(blocks):
        total = total + mm3(s_rows(d), (tap_hi[:, cols], tap_lo[:, cols]), NT)
    for c in range(2):
        outt[c] = total[:, c * TOK : (c + 1) * TOK].reshape(chips, ROWS, TOK)

    def o_send(target, c_, chip_, slot):
        remote(outt.at[c_, chip_], rt.at[home], o_sem.at[0], o_sem.at[1], ctx=target).start()

    everyone(o_send)
    pltpu.make_async_copy(outt.at[core, chip], rt.at[home], o_sem.at[1]).start()

    pltpu.make_async_copy(xb, xb, x_sem.at[1]).wait()
    turn = (
        lax.broadcasted_iota(jnp.int32, (BLOCK, BLOCK), 0) + lax.broadcasted_iota(jnp.int32, (BLOCK, BLOCK), 1) == BLOCK - 1
    ).astype(F32).astype(BF16)
    x_all = jnp.concatenate([xb[0].reshape(chips * ROWS, TOK), xb[1].reshape(chips * ROWS, TOK)], axis=1)
    x_hi, x_lo = split(x_all)
    xr_hi[...] = mm(turn, x_hi, NT).astype(BF16)
    xr_lo[...] = mm(turn, x_lo, NT).astype(BF16)

    for d, cols in enumerate(blocks):
        corr[:, cols] = mm3((xr_hi[...], xr_lo[...]), s_rows(d), NN)

    lined = pltpu.roll(corr[...], wide - (BLOCK - 1), 1, stride=1, stride_axis=0)
    lags = jnp.sum(lined, axis=0, keepdims=True) * scale
    for s in range(fgs.shape[0]):
        fgs[s] = lags[:, s * TOK : (s + 1) * TOK]
    place = lax.rem(chip, 2) * chips + core * (chips // 2) + lax.div(chip, 2)
    share = fg_ref.shape[1]

    def f_send(target, c_, chip_, slot):
        remote(fgs.at[lax.div(chip_ * (2 * share), TOK)], fgr.at[place], f_sem.at[0], f_sem.at[1], ctx=target).start()

    everyone(f_send)
    pltpu.make_async_copy(fgs.at[lax.div(chip * (2 * share), TOK)], fgr.at[place], f_sem.at[1]).start()

    pltpu.make_async_copy(rt, rt, o_sem.at[1]).wait()
    ig_ref[...] = jnp.transpose(rt[...].reshape(n_ctx * ROWS, TOK))
    pltpu.make_async_copy(fgr, fgr, f_sem.at[1]).wait()
    parts = fgr[...].reshape(n_ctx, TOK)
    both = parts[:chips] + parts[chips:]
    offset = lax.rem(me * share, TOK)
    fg_ref[...] = pltpu.roll(both, lax.rem(TOK - offset, TOK), 1)[:, :share]

    pltpu.make_async_copy(wfull.at[pl.ds(0, n_ctx - 1)], wfull.at[pl.ds(0, n_ctx - 1)], w_send).wait()
    if zh_n * x_n > 1:
        sent = cotfull.at[pl.ds(0, zh_n * x_n - 1)]
        pltpu.make_async_copy(sent, sent, c_send).wait()
    for ref, sem in ((xt, x_sem), (st, s_sem), (rt, o_sem), (fgr, f_sem)):
        part = ref.at[pl.ds(0, n_ctx - 1)]
        pltpu.make_async_copy(part, part, sem.at[0]).wait()


def shards(grid, cotangent, out_weight, gate_value, conv_output, conv_input, filters):
    tokens, channels = gate_value.shape
    groups, lag_count = filters.shape
    n_ctx, n_ch = lax.axis_size("ctx"), lax.axis_size("ch")
    chips = n_ctx // 2
    lag_blocks = -(-lag_count // BLOCK)
    wide = (lag_blocks + 1) * BLOCK
    segments = -(-lag_count // TOK)
    scale = 1.0 / math.sqrt(channels // groups * tokens * n_ctx)
    dims = (grid["z_lo"], grid["y"], grid["z_hi"], grid["x"], lag_blocks)
    vmem = pl.BlockSpec(memory_space=pltpu.VMEM)
    dma = pltpu.SemaphoreType.DMA
    return pl.pallas_call(
        functools.partial(kernel, dims, scale),
        out_shape=(
            jax.ShapeDtypeStruct((tokens, channels), F32),
            jax.ShapeDtypeStruct((tokens, channels), F32),
            jax.ShapeDtypeStruct((groups, lag_count // n_ctx), F32),
        ),
        in_specs=[pl.BlockSpec(memory_space=pltpu.HBM)] * 6,
        out_specs=(vmem,) * 3,
        scratch_shapes=[
            pltpu.VMEM((tokens, channels), F32),
            pltpu.VMEM((tokens, channels), F32),
            pltpu.VMEM((tokens, channels), F32),
            pltpu.VMEM((min(8, groups), lag_count), F32),
            pltpu.VMEM((n_ctx, out_weight.shape[1], channels), BF16),
            pltpu.VMEM((n_ch, tokens, channels), BF16),
            pltpu.VMEM((n_ctx, ROWS, TOK), F32),
            pltpu.VMEM((2, chips, ROWS, TOK), F32),
            pltpu.VMEM((n_ctx, ROWS, TOK), F32),
            pltpu.VMEM((2, chips + lag_blocks, ROWS, TOK), F32),
            pltpu.VMEM((2, chips, ROWS, TOK), F32),
            pltpu.VMEM((n_ctx, ROWS, TOK), F32),
            pltpu.VMEM((BLOCK, wide), BF16),
            pltpu.VMEM((BLOCK, wide), BF16),
            pltpu.VMEM((BLOCK, chips * ROWS), BF16),
            pltpu.VMEM((BLOCK, chips * ROWS), BF16),
            pltpu.VMEM((BLOCK, wide), F32),
            pltpu.VMEM((segments, 1, TOK), F32),
            pltpu.VMEM((n_ctx, 1, TOK), F32),
            pltpu.VMEM((tokens, channels), F32),
            dma,
            dma((n_ctx,)),
            dma,
            dma((n_ch,)),
            dma((2,)),
            dma((2,)),
            dma((2,)),
            dma((2,)),
            dma((6,)),
        ],
        compiler_params=pltpu.CompilerParams(
            collective_id=0, has_side_effects=True, vmem_limit_bytes=66_000_000
        ),
    )(cotangent, out_weight.T, gate_value, conv_output, conv_input, filters)


def solution(mesh, grid=GRID):
    return jax.shard_map(
        functools.partial(shards, grid),
        mesh=mesh,
        in_specs=(
            P("ctx", "ch"),
            P("ch", "ctx"),
            P("ctx", "ch"),
            P("ctx", "ch"),
            P("ctx", "ch"),
            P("ch", None),
        ),
        out_specs=(P("ctx", "ch"), P("ctx", "ch"), P("ch", "ctx")),
        check_vma=False,
    )
```

```python
import functools
import math

import jax
import jax.numpy as jnp
from jax import lax
from jax.experimental import pallas as pl
from jax.experimental.pallas import tpu as pltpu
from jax.sharding import PartitionSpec as P

MESH = pl.DeviceIdType.MESH
F32, BF16 = jnp.float32, jnp.bfloat16
NT = (((1,), (1,)), ((), ()))
NN = (((1,), (0,)), ((), ()))
GRID = {"z_lo": 4, "y": 8, "z_hi": 2, "x": 4}
TOK = 128
BLOCK = 2 * TOK
ROWS = 8


def split(value):
    high = value.astype(BF16)
    return high, (value - high.astype(F32)).astype(BF16)


def mm(a, b, dims):
    return lax.dot_general(a, b, dims, preferred_element_type=F32)


def mm3(a, b, dims):
    return mm(a[0], b[0], dims) + (mm(a[0], b[1], dims) + mm(a[1], b[0], dims))


def kernel(
    dims, scale,
    cot_hbm, w_hbm, gate_hbm, cout_hbm, cin_hbm, filt_hbm,
    rt, gg_hbm, fgr,
    gate_ref, cout_ref, cin_ref, filt_ref, wfull, cotfull, gg_ref, xt, xb, st, sb, outt, tap_hi, tap_lo, xr_hi, xr_lo, corr, fgs, grad,
    w_send, w_recv, c_send, c_recv, x_sem, s_sem, o_sem, f_sem, in_sem,
):
    zl_n, y_n, zh_n, x_n, lag_blocks = dims
    chips = zl_n * y_n
    n_ctx = 2 * chips
    me = lax.axis_index("ctx")
    core = lax.rem(me, 2)
    chip = lax.div(me, 2)
    y = lax.rem(chip, y_n)
    zl = lax.div(chip, y_n)
    mej = lax.axis_index("ch")
    x = lax.rem(mej, x_n)
    zh = lax.div(mej, x_n)
    sibling = me + 1 - 2 * core
    x_far = [lax.rem(x + k, x_n) for k in (1, 3, 2) if k < x_n]

    def ctx_of(z_, y_, c_):
        return (z_ * y_n + y_) * 2 + c_

    def remote(src, dst, send, recv, **where):
        return pltpu.make_async_remote_copy(
            src_ref=src, dst_ref=dst, send_sem=send, recv_sem=recv,
            device_id=where, device_id_type=MESH,
        )

    def everyone(send):
        for dy in sorted(range(y_n), key=lambda k: -min(k, y_n - k)):
            for dz in range(zl_n):
                for other in (True, False):
                    if dy or dz or other:
                        c_ = 1 - core if other else core
                        chip_ = z_of[dz] * y_n + y_of[dy]
                        send(2 * chip_ + c_, c_, chip_, c_ * chips + chip_)

    home = core * chips + chip

    barrier = pltpu.get_barrier_semaphore()

    half = y_n // 2
    z_of = [lax.rem(zl + k, zl_n) for k in range(zl_n)]
    y_of = [lax.rem(y + k, y_n) for k in range(y_n)]
    up, down = (ctx_of(zl, y_of[k % y_n], core) for k in (1, y_n - 1))
    rings = [sibling] + ([up, down] if y_n > 2 else [up] * (y_n > 1)) + [ctx_of(z, y, core) for z in z_of[1:]]
    for near in rings:
        pl.semaphore_signal(barrier, inc=1, device_id={"ctx": near}, device_id_type=MESH)
    for near in x_far:
        pl.semaphore_signal(barrier, inc=1, device_id={"ch": zh * x_n + near}, device_id_type=MESH)
    if zh_n > 1:
        pl.semaphore_signal(barrier, inc=1, device_id={"ch": (1 - zh) * x_n + x}, device_id_type=MESH)

    group = core * (chips // 2) + lax.div(chip, 2)
    some = filt_ref.shape[0]
    loads = [
        pltpu.make_async_copy(src, dst, in_sem.at[n])
        for n, (src, dst) in enumerate(
            (
                (cin_hbm, cin_ref),
                (w_hbm, wfull.at[me]),
                (cot_hbm, cotfull.at[mej]),
                (filt_hbm.at[pl.ds(lax.div(group, some) * some, some)], filt_ref),
                (gate_hbm, gate_ref),
                (cout_hbm, cout_ref),
            )
        )
    ]
    for load in loads:
        load.start()
    sb[:, chips:] = jnp.zeros((2, lag_blocks, ROWS, TOK), F32)
    loads[1].wait()
    loads[2].wait()
    depth = w_hbm.shape[0]

    pl.semaphore_wait(barrier, len(rings) + len(x_far) + (zh_n - 1))

    def w_copy(piece, target):
        return remote(wfull.at[piece], wfull.at[piece], w_send, w_recv.at[piece], ctx=target)

    def goes_up(distance, k):
        return distance < half or (distance == half and k < zl_n // 2)

    def goes_down(distance, k):
        return distance < half or (distance == half and k >= zl_n // 2)

    def w_relay(piece, distance, k, to_up, to_down):
        if to_up and goes_up(distance, k):
            w_copy(piece, up).start()
        if to_down and goes_down(distance, k):
            w_copy(piece, down).start()
        w_copy(piece, sibling).start()

    for k in range(1, zl_n):
        w_copy(me, ctx_of(z_of[k], y, core)).start()
    w_relay(me, 1, 0, y_n > 1, y_n > 1)

    def c_copy(piece, xx):
        return remote(cotfull.at[piece], cotfull.at[piece], c_send, c_recv.at[piece], ch=zh * x_n + xx)

    def c_spread(piece):
        for xx in x_far:
            c_copy(piece, xx).start()

    across = (1 - zh) * x_n + x
    c_spread(mej)

    def from_z(k):
        piece = ctx_of(z_of[k], y, core)
        w_copy(piece, sibling).wait_recv()
        w_relay(piece, 1, k, y_n > 1, y_n > 1)

    def from_y(s, k):
        if goes_up(s, k):
            piece = ctx_of(z_of[k], y_of[y_n - s], core)
            w_copy(piece, sibling).wait_recv()
            w_relay(piece, s + 1, k, True, False)
        if goes_down(s, k):
            piece = ctx_of(z_of[k], y_of[s], core)
            w_copy(piece, sibling).wait_recv()
            w_relay(piece, s + 1, k, False, True)

    if half:
        from_y(1, 0)
    for k in range(1, zl_n):
        from_z(k)
    if zh_n > 1:
        remote(cotfull.at[mej], cotfull.at[mej], c_send, c_recv.at[mej], ch=across).start()
    loads[3].wait()
    wide = tap_hi.shape[1]
    row = jnp.pad(filt_ref[pl.ds(lax.rem(group, some), 1), :], ((0, 0), (0, wide - filt_ref.shape[1])))
    taps = pltpu.roll(jnp.broadcast_to(row, (BLOCK, wide)), 0, 1, stride=1, stride_axis=0)
    tap_hi[...], tap_lo[...] = split(taps)

    loads[0].wait()
    xt[...] = jnp.transpose(cin_ref[...]).reshape(n_ctx, ROWS, TOK)
    for s in range(1, half + 1):
        if s < half:
            from_y(s + 1, 0)
        for k in range(1, zl_n):
            from_y(s, k)
        if zh_n > 1 and s == 1:
            c_copy(across, x).wait_recv()
            c_spread(across)
    for piece in range(zh_n * x_n):
        first = lax.rem(mej + piece, zh_n * x_n)
        if piece and zh_n > 1:
            @pl.when(first != across)
            def _():
                c_copy(first, x).wait_recv()
        elif piece:
            c_copy(first, x).wait_recv()

    def from_sibling(q, carry):
        w_copy(2 * q + 1 - core, sibling).wait_recv()
        return carry

    lax.fori_loop(0, chips, from_sibling, 0)

    per = n_ctx // (zh_n * x_n)
    for j in range(zh_n * x_n):
        term = mm(cotfull[j], wfull[pl.ds(j * per, per)].reshape(per * depth, wfull.shape[2]), NN)
        if j == 0:
            grad[...] = term
        else:
            grad[...] += term
    loads[4].wait()
    st[...] = jnp.transpose(grad[...] * gate_ref[...]).reshape(n_ctx, ROWS, TOK)

    def s_send(target, c_, chip_, slot):
        remote(st.at[slot], sb.at[core, chip], s_sem.at[0], s_sem.at[1], ctx=target).start()

    everyone(s_send)
    pltpu.make_async_copy(st.at[home], sb.at[core, chip], s_sem.at[1]).start()

    def x_send(target, c_, chip_, slot):
        remote(xt.at[slot], xb.at[core, chip], x_sem.at[0], x_sem.at[1], ctx=target).start()

    everyone(x_send)
    pltpu.make_async_copy(xt.at[home], xb.at[core, chip], x_sem.at[1]).start()
    loads[5].wait()
    gg_ref[...] = grad[...] * cout_ref[...]
    gate_out = pltpu.make_async_copy(gg_ref, gg_hbm, in_sem.at[0])
    gate_out.start()
    arrived = sb.at[:, pl.ds(0, chips)]
    pltpu.make_async_copy(arrived, arrived, s_sem.at[1]).wait()

    def s_rows(d):
        return split(jnp.concatenate(
            [sb[0, d : d + chips].reshape(chips * ROWS, TOK), sb[1, d : d + chips].reshape(chips * ROWS, TOK)], axis=1
        ))

    blocks = [slice(d * BLOCK, (d + 1) * BLOCK) for d in range(lag_blocks + 1)]
    total = jnp.zeros((chips * ROWS, BLOCK), F32)
    for d, cols in enumerate(blocks):
        total = total + mm3(s_rows(d), (tap_hi[:, cols], tap_lo[:, cols]), NT)
    for c in range(2):
        outt[c] = total[:, c * TOK : (c + 1) * TOK].reshape(chips, ROWS, TOK)

    def o_send(target, c_, chip_, slot):
        remote(outt.at[c_, chip_], rt.at[home], o_sem.at[0], o_sem.at[1], ctx=target).start()

    everyone(o_send)
    pltpu.make_async_copy(outt.at[core, chip], rt.at[home], o_sem.at[1]).start()

    pltpu.make_async_copy(xb, xb, x_sem.at[1]).wait()
    turn = (
        lax.broadcasted_iota(jnp.int32, (BLOCK, BLOCK), 0) + lax.broadcasted_iota(jnp.int32, (BLOCK, BLOCK), 1) == BLOCK - 1
    ).astype(F32).astype(BF16)
    x_all = jnp.concatenate([xb[0].reshape(chips * ROWS, TOK), xb[1].reshape(chips * ROWS, TOK)], axis=1)
    x_hi, x_lo = split(x_all)
    xr_hi[...] = mm(turn, x_hi, NT).astype(BF16)
    xr_lo[...] = mm(turn, x_lo, NT).astype(BF16)

    for d, cols in enumerate(blocks):
        corr[:, cols] = mm3((xr_hi[...], xr_lo[...]), s_rows(d), NN)

    lined = pltpu.roll(corr[...], wide - (BLOCK - 1), 1, stride=1, stride_axis=0)
    lags = jnp.sum(lined, axis=0, keepdims=True) * scale
    for s in range(fgs.shape[0]):
        fgs[s] = lags[:, s * TOK : (s + 1) * TOK]
    place = lax.rem(chip, 2) * chips + core * (chips // 2) + lax.div(chip, 2)
    share = filt_hbm.shape[1] // n_ctx

    def f_send(target, c_, chip_, slot):
        remote(fgs.at[lax.div(chip_ * (2 * share), TOK)], fgr.at[place], f_sem.at[0], f_sem.at[1], ctx=target).start()

    everyone(f_send)
    pltpu.make_async_copy(fgs.at[lax.div(chip * (2 * share), TOK)], fgr.at[place], f_sem.at[1]).start()

    gate_out.wait()
    pltpu.make_async_copy(rt, rt, o_sem.at[1]).wait()
    pltpu.make_async_copy(fgr, fgr, f_sem.at[1]).wait()

    pltpu.make_async_copy(wfull.at[pl.ds(0, n_ctx - 1)], wfull.at[pl.ds(0, n_ctx - 1)], w_send).wait()
    if zh_n * x_n > 1:
        sent = cotfull.at[pl.ds(0, zh_n * x_n - 1)]
        pltpu.make_async_copy(sent, sent, c_send).wait()
    for ref, sem in ((xt, x_sem), (st, s_sem), (rt, o_sem), (fgr, f_sem)):
        part = ref.at[pl.ds(0, n_ctx - 1)]
        pltpu.make_async_copy(part, part, sem.at[0]).wait()


def finish(rt, gg_in, fgr, ig_ref, gg_ref, fg_ref):
    n_ctx = fgr.shape[0]
    ig_ref[...] = jnp.transpose(rt[...].reshape(n_ctx * ROWS, TOK))
    gg_ref[...] = gg_in[...]
    parts = fgr[...].reshape(n_ctx, TOK)
    both = parts[: n_ctx // 2] + parts[n_ctx // 2 :]
    share = fg_ref.shape[1]
    offset = lax.rem(lax.axis_index("ctx") * share, TOK)
    fg_ref[...] = pltpu.roll(both, lax.rem(TOK - offset, TOK), 1)[:, :share]


def shards(grid, cotangent, out_weight, gate_value, conv_output, conv_input, filters):
    tokens, channels = gate_value.shape
    groups, lag_count = filters.shape
    n_ctx, n_ch = lax.axis_size("ctx"), lax.axis_size("ch")
    chips = n_ctx // 2
    lag_blocks = -(-lag_count // BLOCK)
    wide = (lag_blocks + 1) * BLOCK
    segments = -(-lag_count // TOK)
    scale = 1.0 / math.sqrt(channels // groups * tokens * n_ctx)
    dims = (grid["z_lo"], grid["y"], grid["z_hi"], grid["x"], lag_blocks)
    vmem = pl.BlockSpec(memory_space=pltpu.VMEM)
    dma = pltpu.SemaphoreType.DMA
    hbm = pl.BlockSpec(memory_space=pltpu.HBM)
    landed = pl.pallas_call(
        functools.partial(kernel, dims, scale),
        out_shape=(
            jax.ShapeDtypeStruct((n_ctx, ROWS, TOK), F32),
            jax.ShapeDtypeStruct((tokens, channels), F32),
            jax.ShapeDtypeStruct((n_ctx, 1, TOK), F32),
        ),
        in_specs=[hbm] * 6,
        out_specs=(hbm,) * 3,
        scratch_shapes=[
            pltpu.VMEM((tokens, channels), F32),
            pltpu.VMEM((tokens, channels), F32),
            pltpu.VMEM((tokens, channels), F32),
            pltpu.VMEM((min(8, groups), lag_count), F32),
            pltpu.VMEM((n_ctx, out_weight.shape[1], channels), BF16),
            pltpu.VMEM((n_ch, tokens, channels), BF16),
            pltpu.VMEM((tokens, channels), F32),
            pltpu.VMEM((n_ctx, ROWS, TOK), F32),
            pltpu.VMEM((2, chips, ROWS, TOK), F32),
            pltpu.VMEM((n_ctx, ROWS, TOK), F32),
            pltpu.VMEM((2, chips + lag_blocks, ROWS, TOK), F32),
            pltpu.VMEM((2, chips, ROWS, TOK), F32),
            pltpu.VMEM((BLOCK, wide), BF16),
            pltpu.VMEM((BLOCK, wide), BF16),
            pltpu.VMEM((BLOCK, chips * ROWS), BF16),
            pltpu.VMEM((BLOCK, chips * ROWS), BF16),
            pltpu.VMEM((BLOCK, wide), F32),
            pltpu.VMEM((segments, 1, TOK), F32),
            pltpu.VMEM((tokens, channels), F32),
            dma,
            dma((n_ctx,)),
            dma,
            dma((n_ch,)),
            dma((2,)),
            dma((2,)),
            dma((2,)),
            dma((2,)),
            dma((6,)),
        ],
        compiler_params=pltpu.CompilerParams(
            collective_id=0, has_side_effects=True, vmem_limit_bytes=66_000_000
        ),
    )(cotangent, out_weight.T, gate_value, conv_output, conv_input, filters)
    return pl.pallas_call(
        finish,
        out_shape=(
            jax.ShapeDtypeStruct((tokens, channels), F32),
            jax.ShapeDtypeStruct((tokens, channels), F32),
            jax.ShapeDtypeStruct((groups, lag_count // n_ctx), F32),
        ),
        in_specs=[vmem] * 3,
        out_specs=(vmem,) * 3,
        compiler_params=pltpu.CompilerParams(vmem_limit_bytes=66_000_000),
    )(*landed)


def solution(mesh, grid=GRID):
    return jax.shard_map(
        functools.partial(shards, grid),
        mesh=mesh,
        in_specs=(
            P("ctx", "ch"),
            P("ch", "ctx"),
            P("ctx", "ch"),
            P("ctx", "ch"),
            P("ctx", "ch"),
            P("ch", None),
        ),
        out_specs=(P("ctx", "ch"), P("ctx", "ch"), P("ch", "ctx")),
        check_vma=False,
    )
```

```python
import functools
import math

import jax
import jax.numpy as jnp
from jax import lax
from jax.experimental import pallas as pl
from jax.experimental.pallas import tpu as pltpu
from jax.sharding import PartitionSpec as P

MESH = pl.DeviceIdType.MESH
F32, BF16 = jnp.float32, jnp.bfloat16
NT = (((1,), (1,)), ((), ()))
NN = (((1,), (0,)), ((), ()))
GRID = {"z_lo": 4, "y": 8, "z_hi": 2, "x": 4}
TOK = 128
BLOCK = 2 * TOK
ROWS = 8


def split(value):
    high = value.astype(BF16)
    return high, (value - high.astype(F32)).astype(BF16)


def mm(a, b, dims):
    return lax.dot_general(a, b, dims, preferred_element_type=F32)


def mm3(a, b, dims):
    return mm(a[0], b[0], dims) + (mm(a[0], b[1], dims) + mm(a[1], b[0], dims))


def kernel(
    dims, scale,
    cot_hbm, w_hbm, gate_hbm, cout_hbm, cin_hbm, filt_hbm,
    rt, gg_hbm, fgr,
    gate_ref, cout_ref, cin_ref, filt_ref, wfull, cotfull, gg_ref, xt, xb, st, sb, outt, tap_hi, tap_lo, xr_hi, xr_lo, corr, fgs, grad,
    w_send, w_recv, b_send, b_recv, c_send, c_recv, x_sem, s_sem, o_sem, f_sem, in_sem,
):
    zl_n, y_n, zh_n, x_n, lag_blocks = dims
    chips = zl_n * y_n
    depth = w_hbm.shape[0]
    n_ctx = 2 * chips
    me = lax.axis_index("ctx")
    core = lax.rem(me, 2)
    chip = lax.div(me, 2)
    y = lax.rem(chip, y_n)
    zl = lax.div(chip, y_n)
    mej = lax.axis_index("ch")
    x = lax.rem(mej, x_n)
    zh = lax.div(mej, x_n)
    sibling = me + 1 - 2 * core
    x_far = [lax.rem(x + k, x_n) for k in (1, 3, 2) if k < x_n]

    def ctx_of(z_, y_, c_):
        return (z_ * y_n + y_) * 2 + c_

    def remote(src, dst, send, recv, **where):
        return pltpu.make_async_remote_copy(
            src_ref=src, dst_ref=dst, send_sem=send, recv_sem=recv,
            device_id=where, device_id_type=MESH,
        )

    def everyone(send):
        for dy in sorted(range(y_n), key=lambda k: -min(k, y_n - k)):
            for dz in range(zl_n):
                for other in (True, False):
                    if dy or dz or other:
                        c_ = 1 - core if other else core
                        chip_ = z_of[dz] * y_n + y_of[dy]
                        send(2 * chip_ + c_, c_, chip_, c_ * chips + chip_)

    home = core * chips + chip

    barrier = pltpu.get_barrier_semaphore()

    half = y_n // 2
    z_of = [lax.rem(zl + k, zl_n) for k in range(zl_n)]
    y_of = [lax.rem(y + k, y_n) for k in range(y_n)]
    up, down = (ctx_of(zl, y_of[k % y_n], core) for k in (1, y_n - 1))
    y_far = sorted(range(1, y_n), key=lambda k: -min(k, y_n - k))
    rings = [sibling] + [ctx_of(zl, y_of[k], core) for k in y_far] + [ctx_of(z, y, core) for z in z_of[1:]]
    for near in rings:
        pl.semaphore_signal(barrier, inc=1, device_id={"ctx": near}, device_id_type=MESH)
    for near in x_far:
        pl.semaphore_signal(barrier, inc=1, device_id={"ch": zh * x_n + near}, device_id_type=MESH)
    if zh_n > 1:
        pl.semaphore_signal(barrier, inc=1, device_id={"ch": (1 - zh) * x_n + x}, device_id_type=MESH)

    group = core * (chips // 2) + lax.div(chip, 2)
    some = filt_ref.shape[0]
    loads = [
        pltpu.make_async_copy(src, dst, in_sem.at[n])
        for n, (src, dst) in enumerate(
            (
                (cin_hbm, cin_ref),
                (w_hbm, wfull.at[zl, y, core]),
                (cot_hbm, cotfull.at[mej]),
                (filt_hbm.at[pl.ds(lax.div(group, some) * some, some)], filt_ref),
                (gate_hbm, gate_ref),
                (cout_hbm, cout_ref),
            )
        )
    ]
    for load in loads:
        load.start()
    sb[:, chips:] = jnp.zeros((2, lag_blocks, ROWS, TOK), F32)
    loads[1].wait()
    loads[2].wait()

    pl.semaphore_wait(barrier, len(rings) + len(x_far) + (zh_n - 1))

    main = pl.ds(0, depth - depth // 8)
    rest = pl.ds(depth - depth // 8, depth // 8)

    def w_copy(z_, y_, c_, target):
        piece = wfull.at[z_, y_, c_, main]
        return remote(piece, piece, w_send, w_recv.at[z_, y_, c_], ctx=target)

    def goes_up(distance, k):
        return distance < half or (distance == half and k < zl_n // 2)

    def goes_down(distance, k):
        return distance < half or (distance == half and k >= zl_n // 2)

    def w_relay(z_, y_, distance, k, to_up, to_down):
        if to_up and goes_up(distance, k):
            w_copy(z_, y_, core, up).start()
        if to_down and goes_down(distance, k):
            w_copy(z_, y_, core, down).start()
        w_copy(z_, y_, core, sibling).start()

    for k in range(1, zl_n):
        w_copy(zl, y, core, ctx_of(z_of[k], y, core)).start()
    w_relay(zl, y, 1, 0, y_n > 1, y_n > 1)

    def rest_y(y_, target):
        rows = wfull.at[zl, y_, core, rest]
        return remote(rows, rows, b_send, b_recv.at[y_], ctx=target)

    def rest_z(z_, c_, target):
        rows = wfull.at[z_, :, c_, rest]
        return remote(rows, rows, b_send, b_recv.at[y_n + 2 * z_ + c_], ctx=target)

    for k in y_far:
        rest_y(y, ctx_of(zl, y_of[k], core)).start()

    def c_copy(piece, xx):
        return remote(cotfull.at[piece], cotfull.at[piece], c_send, c_recv.at[piece], ch=zh * x_n + xx)

    def c_spread(piece):
        for xx in x_far:
            c_copy(piece, xx).start()

    across = (1 - zh) * x_n + x
    c_spread(mej)

    def from_z(k):
        w_copy(z_of[k], y, core, sibling).wait_recv()
        w_relay(z_of[k], y, 1, k, y_n > 1, y_n > 1)

    def from_y(s, k):
        if goes_up(s, k):
            w_copy(z_of[k], y_of[y_n - s], core, sibling).wait_recv()
            w_relay(z_of[k], y_of[y_n - s], s + 1, k, True, False)
        if goes_down(s, k):
            w_copy(z_of[k], y_of[s], core, sibling).wait_recv()
            w_relay(z_of[k], y_of[s], s + 1, k, False, True)

    if half:
        from_y(1, 0)
    for k in range(1, zl_n):
        from_z(k)
    if zh_n > 1:
        remote(cotfull.at[mej], cotfull.at[mej], c_send, c_recv.at[mej], ch=across).start()
    loads[3].wait()
    wide = tap_hi.shape[1]
    row = jnp.pad(filt_ref[pl.ds(lax.rem(group, some), 1), :], ((0, 0), (0, wide - filt_ref.shape[1])))
    taps = pltpu.roll(jnp.broadcast_to(row, (BLOCK, wide)), 0, 1, stride=1, stride_axis=0)
    tap_hi[...], tap_lo[...] = split(taps)

    loads[0].wait()
    xt[...] = jnp.transpose(cin_ref[...]).reshape(n_ctx, ROWS, TOK)
    for s in range(1, half + 1):
        if s < half:
            from_y(s + 1, 0)
        for k in range(1, zl_n):
            from_y(s, k)
        if s == 1:
            for k in y_far:
                rest_y(y_of[k], sibling).wait_recv()
            for z_ in z_of[1:]:
                rest_z(zl, core, ctx_of(z_, y, core)).start()
            rest_z(zl, core, sibling).start()
        if zh_n > 1 and s == 1:
            c_copy(across, x).wait_recv()
            c_spread(across)
    for z_ in z_of[1:]:
        rest_z(z_, core, sibling).wait_recv()
        rest_z(z_, core, sibling).start()
    for piece in range(zh_n * x_n):
        first = lax.rem(mej + piece, zh_n * x_n)
        if piece and zh_n > 1:
            @pl.when(first != across)
            def _():
                c_copy(first, x).wait_recv()
        elif piece:
            c_copy(first, x).wait_recv()

    for z_ in range(zl_n):
        rest_z(z_, 1 - core, sibling).wait_recv()
        for y_ in range(y_n):
            w_copy(z_, y_, 1 - core, sibling).wait_recv()

    per = n_ctx // (zh_n * x_n)
    for j in range(zh_n * x_n):
        z_, y_ = divmod(j * per // 2, y_n)
        whole = per // 2 % y_n == 0
        rows = wfull[z_ : z_ + per // 2 // y_n] if whole else wfull[z_, y_ : y_ + per // 2]
        term = mm(cotfull[j], rows.reshape(per * depth, wfull.shape[4]), NN)
        if j == 0:
            grad[...] = term
        else:
            grad[...] += term
    loads[4].wait()
    st[...] = jnp.transpose(grad[...] * gate_ref[...]).reshape(n_ctx, ROWS, TOK)

    def s_send(target, c_, chip_, slot):
        remote(st.at[slot], sb.at[core, chip], s_sem.at[0], s_sem.at[1], ctx=target).start()

    everyone(s_send)
    pltpu.make_async_copy(st.at[home], sb.at[core, chip], s_sem.at[1]).start()

    def x_send(target, c_, chip_, slot):
        remote(xt.at[slot], xb.at[core, chip], x_sem.at[0], x_sem.at[1], ctx=target).start()

    everyone(x_send)
    pltpu.make_async_copy(xt.at[home], xb.at[core, chip], x_sem.at[1]).start()
    loads[5].wait()
    gg_ref[...] = grad[...] * cout_ref[...]
    gate_out = pltpu.make_async_copy(gg_ref, gg_hbm, in_sem.at[0])
    gate_out.start()
    arrived = sb.at[:, pl.ds(0, chips)]
    pltpu.make_async_copy(arrived, arrived, s_sem.at[1]).wait()

    def s_rows(d):
        return split(jnp.concatenate(
            [sb[0, d : d + chips].reshape(chips * ROWS, TOK), sb[1, d : d + chips].reshape(chips * ROWS, TOK)], axis=1
        ))

    blocks = [slice(d * BLOCK, (d + 1) * BLOCK) for d in range(lag_blocks + 1)]
    total = jnp.zeros((chips * ROWS, BLOCK), F32)
    for d, cols in enumerate(blocks):
        total = total + mm3(s_rows(d), (tap_hi[:, cols], tap_lo[:, cols]), NT)
    for c in range(2):
        outt[c] = total[:, c * TOK : (c + 1) * TOK].reshape(chips, ROWS, TOK)

    def o_send(target, c_, chip_, slot):
        remote(outt.at[c_, chip_], rt.at[home], o_sem.at[0], o_sem.at[1], ctx=target).start()

    everyone(o_send)
    pltpu.make_async_copy(outt.at[core, chip], rt.at[home], o_sem.at[1]).start()

    pltpu.make_async_copy(xb, xb, x_sem.at[1]).wait()
    turn = (
        lax.broadcasted_iota(jnp.int32, (BLOCK, BLOCK), 0) + lax.broadcasted_iota(jnp.int32, (BLOCK, BLOCK), 1) == BLOCK - 1
    ).astype(F32).astype(BF16)
    x_all = jnp.concatenate([xb[0].reshape(chips * ROWS, TOK), xb[1].reshape(chips * ROWS, TOK)], axis=1)
    x_hi, x_lo = split(x_all)
    xr_hi[...] = mm(turn, x_hi, NT).astype(BF16)
    xr_lo[...] = mm(turn, x_lo, NT).astype(BF16)

    for d, cols in enumerate(blocks):
        corr[:, cols] = mm3((xr_hi[...], xr_lo[...]), s_rows(d), NN)

    lined = pltpu.roll(corr[...], wide - (BLOCK - 1), 1, stride=1, stride_axis=0)
    lags = jnp.sum(lined, axis=0, keepdims=True) * scale
    for s in range(fgs.shape[0]):
        fgs[s] = lags[:, s * TOK : (s + 1) * TOK]
    place = lax.rem(chip, 2) * chips + core * (chips // 2) + lax.div(chip, 2)
    share = filt_hbm.shape[1] // n_ctx

    def f_send(target, c_, chip_, slot):
        remote(fgs.at[lax.div(chip_ * (2 * share), TOK)], fgr.at[place], f_sem.at[0], f_sem.at[1], ctx=target).start()

    everyone(f_send)
    pltpu.make_async_copy(fgs.at[lax.div(chip * (2 * share), TOK)], fgr.at[place], f_sem.at[1]).start()

    gate_out.wait()
    pltpu.make_async_copy(rt, rt, o_sem.at[1]).wait()
    pltpu.make_async_copy(fgr, fgr, f_sem.at[1]).wait()

    left = [(w_send, wfull.at[0, 0, 0, main])]
    if y_n > 1:
        left += [(w_send, wfull.at[0, pl.ds(0, y_n - 1), :, main]), (b_send, wfull.at[0, pl.ds(0, y_n - 1), 0, rest])]
    if zl_n > 1:
        left += [(w_send, wfull.at[pl.ds(0, zl_n - 1), :, :, main]), (b_send, wfull.at[pl.ds(0, zl_n - 1), :, 0, rest])]
    left += [(b_send, wfull.at[:, :, 0, rest])]
    for sem, part in left:
        pltpu.make_async_copy(part, part, sem).wait()
    if zh_n * x_n > 1:
        sent = cotfull.at[pl.ds(0, zh_n * x_n - 1)]
        pltpu.make_async_copy(sent, sent, c_send).wait()
    for ref, sem in ((xt, x_sem), (st, s_sem), (rt, o_sem), (fgr, f_sem)):
        part = ref.at[pl.ds(0, n_ctx - 1)]
        pltpu.make_async_copy(part, part, sem.at[0]).wait()


def finish(rt, gg_in, fgr, ig_ref, gg_ref, fg_ref):
    n_ctx = fgr.shape[0]
    ig_ref[...] = jnp.transpose(rt[...].reshape(n_ctx * ROWS, TOK))
    gg_ref[...] = gg_in[...]
    parts = fgr[...].reshape(n_ctx, TOK)
    both = parts[: n_ctx // 2] + parts[n_ctx // 2 :]
    share = fg_ref.shape[1]
    offset = lax.rem(lax.axis_index("ctx") * share, TOK)
    fg_ref[...] = pltpu.roll(both, lax.rem(TOK - offset, TOK), 1)[:, :share]


def shards(grid, cotangent, out_weight, gate_value, conv_output, conv_input, filters):
    tokens, channels = gate_value.shape
    groups, lag_count = filters.shape
    n_ctx, n_ch = lax.axis_size("ctx"), lax.axis_size("ch")
    chips = n_ctx // 2
    lag_blocks = -(-lag_count // BLOCK)
    wide = (lag_blocks + 1) * BLOCK
    segments = -(-lag_count // TOK)
    scale = 1.0 / math.sqrt(channels // groups * tokens * n_ctx)
    dims = (grid["z_lo"], grid["y"], grid["z_hi"], grid["x"], lag_blocks)
    vmem = pl.BlockSpec(memory_space=pltpu.VMEM)
    dma = pltpu.SemaphoreType.DMA
    hbm = pl.BlockSpec(memory_space=pltpu.HBM)
    landed = pl.pallas_call(
        functools.partial(kernel, dims, scale),
        out_shape=(
            jax.ShapeDtypeStruct((n_ctx, ROWS, TOK), F32),
            jax.ShapeDtypeStruct((tokens, channels), F32),
            jax.ShapeDtypeStruct((n_ctx, 1, TOK), F32),
        ),
        in_specs=[hbm] * 6,
        out_specs=(hbm,) * 3,
        scratch_shapes=[
            pltpu.VMEM((tokens, channels), F32),
            pltpu.VMEM((tokens, channels), F32),
            pltpu.VMEM((tokens, channels), F32),
            pltpu.VMEM((min(8, groups), lag_count), F32),
            pltpu.VMEM((grid["z_lo"], grid["y"], 2, out_weight.shape[1], channels), BF16),
            pltpu.VMEM((n_ch, tokens, channels), BF16),
            pltpu.VMEM((tokens, channels), F32),
            pltpu.VMEM((n_ctx, ROWS, TOK), F32),
            pltpu.VMEM((2, chips, ROWS, TOK), F32),
            pltpu.VMEM((n_ctx, ROWS, TOK), F32),
            pltpu.VMEM((2, chips + lag_blocks, ROWS, TOK), F32),
            pltpu.VMEM((2, chips, ROWS, TOK), F32),
            pltpu.VMEM((BLOCK, wide), BF16),
            pltpu.VMEM((BLOCK, wide), BF16),
            pltpu.VMEM((BLOCK, chips * ROWS), BF16),
            pltpu.VMEM((BLOCK, chips * ROWS), BF16),
            pltpu.VMEM((BLOCK, wide), F32),
            pltpu.VMEM((segments, 1, TOK), F32),
            pltpu.VMEM((tokens, channels), F32),
            dma,
            dma((grid["z_lo"], grid["y"], 2)),
            dma,
            dma((grid["y"] + 2 * grid["z_lo"],)),
            dma,
            dma((n_ch,)),
            dma((2,)),
            dma((2,)),
            dma((2,)),
            dma((2,)),
            dma((6,)),
        ],
        compiler_params=pltpu.CompilerParams(
            collective_id=0, has_side_effects=True, vmem_limit_bytes=66_000_000
        ),
    )(cotangent, out_weight.T, gate_value, conv_output, conv_input, filters)
    return pl.pallas_call(
        finish,
        out_shape=(
            jax.ShapeDtypeStruct((tokens, channels), F32),
            jax.ShapeDtypeStruct((tokens, channels), F32),
            jax.ShapeDtypeStruct((groups, lag_count // n_ctx), F32),
        ),
        in_specs=[vmem] * 3,
        out_specs=(vmem,) * 3,
        compiler_params=pltpu.CompilerParams(vmem_limit_bytes=66_000_000),
    )(*landed)


def solution(mesh, grid=GRID):
    return jax.shard_map(
        functools.partial(shards, grid),
        mesh=mesh,
        in_specs=(
            P("ctx", "ch"),
            P("ch", "ctx"),
            P("ctx", "ch"),
            P("ctx", "ch"),
            P("ctx", "ch"),
            P("ch", None),
        ),
        out_specs=(P("ctx", "ch"), P("ctx", "ch"), P("ch", "ctx")),
        check_vma=False,
    )
```

```python
import functools
import math

import jax
import jax.numpy as jnp
from jax import lax
from jax.experimental import pallas as pl
from jax.experimental.pallas import tpu as pltpu
from jax.sharding import PartitionSpec as P

MESH = pl.DeviceIdType.MESH
F32, BF16 = jnp.float32, jnp.bfloat16
NT = (((1,), (1,)), ((), ()))
NN = (((1,), (0,)), ((), ()))
GRID = {"z_lo": 4, "y": 8, "z_hi": 2, "x": 4}
TOK = 128
BLOCK = 2 * TOK
ROWS = 8


def split(value):
    high = value.astype(BF16)
    return high, (value - high.astype(F32)).astype(BF16)


def mm(a, b, dims):
    return lax.dot_general(a, b, dims, preferred_element_type=F32)


def mm3(a, b, dims):
    return mm(a[0], b[0], dims) + (mm(a[0], b[1], dims) + mm(a[1], b[0], dims))


def kernel(
    dims, scale,
    cot_hbm, w_hbm, gate_hbm, cout_hbm, cin_hbm, filt_hbm,
    rt, gg_hbm, fgr,
    gate_ref, cout_ref, cin_ref, filt_ref, wfull, cotfull, gg_ref, xt, xb, st, sb, outt, tap_hi, tap_lo, xr_hi, xr_lo, corr, s_hi, s_lo, fgs, grad,
    w_send, w_recv, b_send, b_recv, c_send, c_recv, x_sem, s_sem, o_sem, f_sem, in_sem,
):
    zl_n, y_n, zh_n, x_n, lag_blocks = dims
    chips = zl_n * y_n
    depth = w_hbm.shape[0]
    n_ctx = 2 * chips
    me = lax.axis_index("ctx")
    core = lax.rem(me, 2)
    chip = lax.div(me, 2)
    y = lax.rem(chip, y_n)
    zl = lax.div(chip, y_n)
    mej = lax.axis_index("ch")
    x = lax.rem(mej, x_n)
    zh = lax.div(mej, x_n)
    sibling = me + 1 - 2 * core
    x_far = [lax.rem(x + k, x_n) for k in (1, 3, 2) if k < x_n]

    def ctx_of(z_, y_, c_):
        return (z_ * y_n + y_) * 2 + c_

    def remote(src, dst, send, recv, **where):
        return pltpu.make_async_remote_copy(
            src_ref=src, dst_ref=dst, send_sem=send, recv_sem=recv,
            device_id=where, device_id_type=MESH,
        )

    def everyone(send):
        for dy in sorted(range(y_n), key=lambda k: -min(k, y_n - k)):
            for dz in range(zl_n):
                for other in (True, False):
                    if dy or dz or other:
                        c_ = 1 - core if other else core
                        chip_ = z_of[dz] * y_n + y_of[dy]
                        send(2 * chip_ + c_, c_, chip_, c_ * chips + chip_)

    home = core * chips + chip

    barrier = pltpu.get_barrier_semaphore()

    half = y_n // 2
    z_of = [lax.rem(zl + k, zl_n) for k in range(zl_n)]
    y_of = [lax.rem(y + k, y_n) for k in range(y_n)]
    up, down = (ctx_of(zl, y_of[k % y_n], core) for k in (1, y_n - 1))
    y_far = sorted(range(1, y_n), key=lambda k: -min(k, y_n - k))
    rings = [sibling] + [ctx_of(zl, y_of[k], core) for k in y_far] + [ctx_of(z, y, core) for z in z_of[1:]]
    for near in rings:
        pl.semaphore_signal(barrier, inc=1, device_id={"ctx": near}, device_id_type=MESH)
    for near in x_far:
        pl.semaphore_signal(barrier, inc=1, device_id={"ch": zh * x_n + near}, device_id_type=MESH)
    if zh_n > 1:
        pl.semaphore_signal(barrier, inc=1, device_id={"ch": (1 - zh) * x_n + x}, device_id_type=MESH)

    group = core * (chips // 2) + lax.div(chip, 2)
    some = filt_ref.shape[0]
    loads = [
        pltpu.make_async_copy(src, dst, in_sem.at[n])
        for n, (src, dst) in enumerate(
            (
                (cin_hbm, cin_ref),
                (w_hbm, wfull.at[zl, y, core]),
                (cot_hbm, cotfull.at[mej]),
                (filt_hbm.at[pl.ds(lax.div(group, some) * some, some)], filt_ref),
                (gate_hbm, gate_ref),
                (cout_hbm, cout_ref),
            )
        )
    ]
    for load in loads:
        load.start()
    wide = tap_hi.shape[1]
    sb[:, chips:] = jnp.zeros((2, lag_blocks, ROWS, TOK), F32)
    loads[1].wait()
    loads[2].wait()

    pl.semaphore_wait(barrier, len(rings) + len(x_far) + (zh_n - 1))

    main = pl.ds(0, depth - depth // 8)
    rest = pl.ds(depth - depth // 8, depth // 8)

    def w_copy(z_, y_, c_, target):
        piece = wfull.at[z_, y_, c_, main]
        return remote(piece, piece, w_send, w_recv.at[z_, y_, c_], ctx=target)

    def goes_up(distance, k):
        return distance < half or (distance == half and k < zl_n // 2)

    def goes_down(distance, k):
        return distance < half or (distance == half and k >= zl_n // 2)

    def w_relay(z_, y_, distance, k, to_up, to_down):
        if to_up and goes_up(distance, k):
            w_copy(z_, y_, core, up).start()
        if to_down and goes_down(distance, k):
            w_copy(z_, y_, core, down).start()
        w_copy(z_, y_, core, sibling).start()

    for k in range(1, zl_n):
        w_copy(zl, y, core, ctx_of(z_of[k], y, core)).start()
    w_relay(zl, y, 1, 0, y_n > 1, y_n > 1)

    def rest_y(y_, target):
        rows = wfull.at[zl, y_, core, rest]
        return remote(rows, rows, b_send, b_recv.at[y_], ctx=target)

    def rest_z(z_, c_, target):
        rows = wfull.at[z_, :, c_, rest]
        return remote(rows, rows, b_send, b_recv.at[y_n + 2 * z_ + c_], ctx=target)

    for k in y_far:
        rest_y(y, ctx_of(zl, y_of[k], core)).start()

    def c_copy(piece, xx):
        return remote(cotfull.at[piece], cotfull.at[piece], c_send, c_recv.at[piece], ch=zh * x_n + xx)

    def c_spread(piece):
        for xx in x_far:
            c_copy(piece, xx).start()

    across = (1 - zh) * x_n + x
    c_spread(mej)

    def from_z(k):
        w_copy(z_of[k], y, core, sibling).wait_recv()
        w_relay(z_of[k], y, 1, k, y_n > 1, y_n > 1)

    def from_y(s, k):
        if goes_up(s, k):
            w_copy(z_of[k], y_of[y_n - s], core, sibling).wait_recv()
            w_relay(z_of[k], y_of[y_n - s], s + 1, k, True, False)
        if goes_down(s, k):
            w_copy(z_of[k], y_of[s], core, sibling).wait_recv()
            w_relay(z_of[k], y_of[s], s + 1, k, False, True)

    if half:
        from_y(1, 0)
    for k in range(1, zl_n):
        from_z(k)
    if zh_n > 1:
        remote(cotfull.at[mej], cotfull.at[mej], c_send, c_recv.at[mej], ch=across).start()
    for s in range(1, half + 1):
        if s < half:
            from_y(s + 1, 0)
        for k in range(1, zl_n):
            from_y(s, k)
        if s == 1:
            for k in y_far:
                rest_y(y_of[k], sibling).wait_recv()
            for z_ in z_of[1:]:
                rest_z(zl, core, ctx_of(z_, y, core)).start()
            rest_z(zl, core, sibling).start()
        if s == min(2, half):
            loads[3].wait()
            wide = tap_hi.shape[1]
            row = jnp.pad(filt_ref[pl.ds(lax.rem(group, some), 1), :], ((0, 0), (0, wide - filt_ref.shape[1])))
            taps = pltpu.roll(jnp.broadcast_to(row, (BLOCK, wide)), 0, 1, stride=1, stride_axis=0)
            tap_hi[...], tap_lo[...] = split(taps)

            loads[0].wait()
            xt[...] = jnp.transpose(cin_ref[...]).reshape(n_ctx, ROWS, TOK)
        if zh_n > 1 and s == 1:
            c_copy(across, x).wait_recv()
            c_spread(across)
    for z_ in z_of[1:]:
        rest_z(z_, core, sibling).wait_recv()
        rest_z(z_, core, sibling).start()
    for piece in range(zh_n * x_n):
        first = lax.rem(mej + piece, zh_n * x_n)
        if piece and zh_n > 1:
            @pl.when(first != across)
            def _():
                c_copy(first, x).wait_recv()
        elif piece:
            c_copy(first, x).wait_recv()

    for z_ in range(zl_n):
        rest_z(z_, 1 - core, sibling).wait_recv()
        for y_ in range(y_n):
            w_copy(z_, y_, 1 - core, sibling).wait_recv()

    per = n_ctx // (zh_n * x_n)
    for j in range(zh_n * x_n):
        z_, y_ = divmod(j * per // 2, y_n)
        whole = per // 2 % y_n == 0
        rows = wfull[z_ : z_ + per // 2 // y_n] if whole else wfull[z_, y_ : y_ + per // 2]
        term = mm(cotfull[j], rows.reshape(per * depth, wfull.shape[4]), NN)
        if j == 0:
            grad[...] = term
        else:
            grad[...] += term
    loads[4].wait()
    st[...] = jnp.transpose(grad[...] * gate_ref[...]).reshape(n_ctx, ROWS, TOK)

    def s_send(target, c_, chip_, slot):
        remote(st.at[slot], sb.at[core, chip], s_sem.at[0], s_sem.at[1], ctx=target).start()

    everyone(s_send)
    pltpu.make_async_copy(st.at[home], sb.at[core, chip], s_sem.at[1]).start()

    def x_send(target, c_, chip_, slot):
        remote(xt.at[slot], xb.at[core, chip], x_sem.at[0], x_sem.at[1], ctx=target).start()

    everyone(x_send)
    pltpu.make_async_copy(xt.at[home], xb.at[core, chip], x_sem.at[1]).start()
    loads[5].wait()
    gg_ref[...] = grad[...] * cout_ref[...]
    gate_out = pltpu.make_async_copy(gg_ref, gg_hbm, in_sem.at[0])
    gate_out.start()
    arrived = sb.at[:, pl.ds(0, chips)]
    pltpu.make_async_copy(arrived, arrived, s_sem.at[1]).wait()

    def s_rows(d):
        return split(jnp.concatenate(
            [sb[0, d : d + chips].reshape(chips * ROWS, TOK), sb[1, d : d + chips].reshape(chips * ROWS, TOK)], axis=1
        ))

    blocks = [slice(d * BLOCK, (d + 1) * BLOCK) for d in range(lag_blocks + 1)]
    total = jnp.zeros((chips * ROWS, BLOCK), F32)
    for d, cols in enumerate(blocks):
        s_hi[d], s_lo[d] = pair = s_rows(d)
        total = total + mm3(pair, (tap_hi[:, cols], tap_lo[:, cols]), NT)
    for c in range(2):
        outt[c] = total[:, c * TOK : (c + 1) * TOK].reshape(chips, ROWS, TOK)

    def o_send(target, c_, chip_, slot):
        remote(outt.at[c_, chip_], rt.at[home], o_sem.at[0], o_sem.at[1], ctx=target).start()

    everyone(o_send)
    pltpu.make_async_copy(outt.at[core, chip], rt.at[home], o_sem.at[1]).start()

    pltpu.make_async_copy(xb, xb, x_sem.at[1]).wait()
    turn = (
        lax.broadcasted_iota(jnp.int32, (BLOCK, BLOCK), 0) + lax.broadcasted_iota(jnp.int32, (BLOCK, BLOCK), 1) == BLOCK - 1
    ).astype(F32).astype(BF16)
    x_all = jnp.concatenate([xb[0].reshape(chips * ROWS, TOK), xb[1].reshape(chips * ROWS, TOK)], axis=1)
    x_hi, x_lo = split(x_all)
    xr_hi[...] = mm(turn, x_hi, NT).astype(BF16)
    xr_lo[...] = mm(turn, x_lo, NT).astype(BF16)

    for d, cols in enumerate(blocks):
        corr[:, cols] = mm3((xr_hi[...], xr_lo[...]), (s_hi[d], s_lo[d]), NN)

    folded = corr[TOK:, : wide - TOK] + corr[:TOK, TOK:]
    lined = pltpu.roll(folded, wide - TOK - (TOK - 1), 1, stride=1, stride_axis=0)
    lags = jnp.sum(lined, axis=0, keepdims=True) * scale
    for s in range(fgs.shape[0]):
        fgs[s] = lags[:, s * TOK : (s + 1) * TOK]
    place = lax.rem(chip, 2) * chips + core * (chips // 2) + lax.div(chip, 2)
    share = filt_hbm.shape[1] // n_ctx

    def f_send(target, c_, chip_, slot):
        remote(fgs.at[lax.div(chip_ * (2 * share), TOK)], fgr.at[place], f_sem.at[0], f_sem.at[1], ctx=target).start()

    everyone(f_send)
    pltpu.make_async_copy(fgs.at[lax.div(chip * (2 * share), TOK)], fgr.at[place], f_sem.at[1]).start()

    gate_out.wait()
    pltpu.make_async_copy(rt, rt, o_sem.at[1]).wait()
    pltpu.make_async_copy(fgr, fgr, f_sem.at[1]).wait()

    left = [(w_send, wfull.at[0, 0, 0, main])]
    if y_n > 1:
        left += [(w_send, wfull.at[0, pl.ds(0, y_n - 1), :, main]), (b_send, wfull.at[0, pl.ds(0, y_n - 1), 0, rest])]
    if zl_n > 1:
        left += [(w_send, wfull.at[pl.ds(0, zl_n - 1), :, :, main]), (b_send, wfull.at[pl.ds(0, zl_n - 1), :, 0, rest])]
    left += [(b_send, wfull.at[:, :, 0, rest])]
    for sem, part in left:
        pltpu.make_async_copy(part, part, sem).wait()
    if zh_n * x_n > 1:
        sent = cotfull.at[pl.ds(0, zh_n * x_n - 1)]
        pltpu.make_async_copy(sent, sent, c_send).wait()
    for ref, sem in ((xt, x_sem), (st, s_sem), (rt, o_sem), (fgr, f_sem)):
        part = ref.at[pl.ds(0, n_ctx - 1)]
        pltpu.make_async_copy(part, part, sem.at[0]).wait()


def finish(rt, gg_in, fgr, ig_ref, gg_ref, fg_ref):
    n_ctx = fgr.shape[0]
    ig_ref[...] = jnp.transpose(rt[...].reshape(n_ctx * ROWS, TOK))
    gg_ref[...] = gg_in[...]
    parts = fgr[...].reshape(n_ctx, TOK)
    both = parts[: n_ctx // 2] + parts[n_ctx // 2 :]
    share = fg_ref.shape[1]
    offset = lax.rem(lax.axis_index("ctx") * share, TOK)
    fg_ref[...] = pltpu.roll(both, lax.rem(TOK - offset, TOK), 1)[:, :share]


def shards(grid, cotangent, out_weight, gate_value, conv_output, conv_input, filters):
    tokens, channels = gate_value.shape
    groups, lag_count = filters.shape
    n_ctx, n_ch = lax.axis_size("ctx"), lax.axis_size("ch")
    chips = n_ctx // 2
    lag_blocks = -(-lag_count // BLOCK)
    wide = (lag_blocks + 1) * BLOCK
    segments = -(-lag_count // TOK)
    scale = 1.0 / math.sqrt(channels // groups * tokens * n_ctx)
    dims = (grid["z_lo"], grid["y"], grid["z_hi"], grid["x"], lag_blocks)
    vmem = pl.BlockSpec(memory_space=pltpu.VMEM)
    dma = pltpu.SemaphoreType.DMA
    hbm = pl.BlockSpec(memory_space=pltpu.HBM)
    landed = pl.pallas_call(
        functools.partial(kernel, dims, scale),
        out_shape=(
            jax.ShapeDtypeStruct((n_ctx, ROWS, TOK), F32),
            jax.ShapeDtypeStruct((tokens, channels), F32),
            jax.ShapeDtypeStruct((n_ctx, 1, TOK), F32),
        ),
        in_specs=[hbm] * 6,
        out_specs=(hbm,) * 3,
        scratch_shapes=[
            pltpu.VMEM((tokens, channels), F32),
            pltpu.VMEM((tokens, channels), F32),
            pltpu.VMEM((tokens, channels), F32),
            pltpu.VMEM((min(8, groups), lag_count), F32),
            pltpu.VMEM((grid["z_lo"], grid["y"], 2, out_weight.shape[1], channels), BF16),
            pltpu.VMEM((n_ch, tokens, channels), BF16),
            pltpu.VMEM((tokens, channels), F32),
            pltpu.VMEM((n_ctx, ROWS, TOK), F32),
            pltpu.VMEM((2, chips, ROWS, TOK), F32),
            pltpu.VMEM((n_ctx, ROWS, TOK), F32),
            pltpu.VMEM((2, chips + lag_blocks, ROWS, TOK), F32),
            pltpu.VMEM((2, chips, ROWS, TOK), F32),
            pltpu.VMEM((BLOCK, wide), BF16),
            pltpu.VMEM((BLOCK, wide), BF16),
            pltpu.VMEM((BLOCK, chips * ROWS), BF16),
            pltpu.VMEM((BLOCK, chips * ROWS), BF16),
            pltpu.VMEM((BLOCK, wide), F32),
            pltpu.VMEM((lag_blocks + 1, chips * ROWS, BLOCK), BF16),
            pltpu.VMEM((lag_blocks + 1, chips * ROWS, BLOCK), BF16),
            pltpu.VMEM((segments, 1, TOK), F32),
            pltpu.VMEM((tokens, channels), F32),
            dma,
            dma((grid["z_lo"], grid["y"], 2)),
            dma,
            dma((grid["y"] + 2 * grid["z_lo"],)),
            dma,
            dma((n_ch,)),
            dma((2,)),
            dma((2,)),
            dma((2,)),
            dma((2,)),
            dma((6,)),
        ],
        compiler_params=pltpu.CompilerParams(
            collective_id=0, has_side_effects=True, vmem_limit_bytes=66_000_000
        ),
    )(cotangent, out_weight.T, gate_value, conv_output, conv_input, filters)
    return pl.pallas_call(
        finish,
        out_shape=(
            jax.ShapeDtypeStruct((tokens, channels), F32),
            jax.ShapeDtypeStruct((tokens, channels), F32),
            jax.ShapeDtypeStruct((groups, lag_count // n_ctx), F32),
        ),
        in_specs=[vmem] * 3,
        out_specs=(vmem,) * 3,
        compiler_params=pltpu.CompilerParams(vmem_limit_bytes=66_000_000),
    )(*landed)


def solution(mesh, grid=GRID):
    return jax.shard_map(
        functools.partial(shards, grid),
        mesh=mesh,
        in_specs=(
            P("ctx", "ch"),
            P("ch", "ctx"),
            P("ctx", "ch"),
            P("ctx", "ch"),
            P("ctx", "ch"),
            P("ch", None),
        ),
        out_specs=(P("ctx", "ch"), P("ctx", "ch"), P("ch", "ctx")),
        check_vma=False,
    )
```
